512 devices in a mesh: row: 32 (over y, z_lo, core), col: 16 (over x, z_hi).
Axes of the slice: x: 4, y: 8, z: 8 (z_hi: 4, z_lo: 2; z = z_hi * 2 + z_lo), core: 2. Of those that a mesh axis runs over, the one named last changes fastest.
Arguments:
- queries: bfloat16 [65536, 512], P(('row', 'col')), may hold values from -6 to 6
- grad_out: bfloat16 [65536, 512], P(('row', 'col')), may hold values from -6 to 6
- attn_out: bfloat16 [65536, 512], P(('row', 'col')), may hold values from -2 to 2
- key_states: bfloat16 [65536, 128], P(('row', 'col')), may hold values from -6 to 6
- value_states: bfloat16 [65536, 128], P(('row', 'col')), may hold values from -2 to 2
- log_norm: float32 [65536, 4], P(('row', 'col')), as said below
- position: int32 [65536], replicated, may hold values from 0 to 8191, as said below
- modality: int32 [65536], replicated, may hold values from 0 to 2, as said below
- bidirectional: int32 [3, 3], replicated, may hold values from 0 to 1
Outputs:
- grad_query: bfloat16 [65536, 512], P(('row', 'col'))
- grad_key: bfloat16 [65536, 128], P(('row', 'col'))
- grad_value: bfloat16 [65536, 128], P(('row', 'col'))
The draws below stay inside these ranges and needn't reach their ends.
Inputs may be any that keep to these rules, and one draw needn't show every extreme that they name: `position`: within each sequence a permutation of 0 to 8191, token t belonging to sequence (t // 128) % 16 // 2; the tokens of one device hold two runs of 64 consecutive positions. `modality`: the same for all tokens of one sequence within one span of 32 consecutive positions. `log_norm`: the log of the number of keys that the token may see, plus 0.25 to 0.75.
All inputs are finite; a program needn't handle non-finite values.
Results may differ from the reference program's by a relative error of at most 0.0052.
Values may be sent and summed in bfloat16 or wider, within the bound.
No kernel may reach another device: no remote copies, remote signals or barrier semaphores. Data moves between devices by JAX's collectives and lax.ppermute only.
A program may use at most 64 MiB of HBM per device.

```python
import functools
import math
import jax
import jax.numpy as jnp
from jax import lax

HEADS = 4
HEAD_DIM = 128
TOK_DEV = 128
SEQS = 8
SEQ_LEN = 8192
TOKENS = 65536
UNIT = 64
SPAN = 32
N_ROW = 32


def shared_layout(key):
    base = jax.random.fold_in(key, 4242)
    key_order, key_mod, key_table = jax.random.split(base, 3)
    block_count = SEQ_LEN // TOK_DEV

    def one_order(order_key):
        return jax.random.permutation(order_key, block_count)
    order = jax.vmap(one_order)(jax.random.split(key_order, SEQS)).astype(jnp.int32)
    token = jnp.arange(TOKENS, dtype=jnp.int32)
    block = token // TOK_DEV
    seq_tok = block % (2 * SEQS) // 2
    local_block = block // (2 * SEQS) * 2 + block % 2
    offset = token % TOK_DEV
    first = order[seq_tok, local_block]
    position = jnp.where(offset < UNIT, first * UNIT + offset, (2 * block_count - 1 - first) * UNIT + offset - UNIT)
    span_mod = jax.random.randint(key_mod, (SEQS, SEQ_LEN // SPAN + 1), 0, 3, dtype=jnp.int32)
    pos_mod = span_mod[:, jnp.arange(SEQ_LEN, dtype=jnp.int32) // SPAN]
    modality = pos_mod[seq_tok, position]
    table = jax.random.randint(key_table, (3, 3), 0, 2, dtype=jnp.int32)
    table = table.at[0, 0].set(0).at[1, 1].set(1)
    return (position.astype(jnp.int32), modality.astype(jnp.int32), table, pos_mod, seq_tok)


def draw_position(key, part):
    return shared_layout(key)[0]


def draw_modality(key, part):
    return shared_layout(key)[1]


def draw_bidirectional(key, part):
    return shared_layout(key)[2]


def draw_log_norm(key, part):
    position, modality, table, pos_mod, seq_tok = shared_layout(key)
    unit_mod = pos_mod.reshape(SEQS, SEQ_LEN // UNIT, UNIT)
    slots = jnp.arange(UNIT, dtype=jnp.int32)
    later = slots[None, :] > slots[:, None]
    pair = table[unit_mod[:, :, :, None], unit_mod[:, :, None, :]] == 1
    extra = jnp.sum(jnp.where(later[None, None, :, :] & pair, 1, 0), axis=3).reshape(SEQS, SEQ_LEN)
    count_pos = jnp.arange(SEQ_LEN, dtype=jnp.int32)[None, :] + 1 + extra
    count_tok = count_pos[seq_tok, position]
    noise = jax.random.uniform(jax.random.fold_in(key, 99), (TOKENS, HEADS), jnp.float32, -0.25, 0.25)
    return jnp.log(count_tok.astype(jnp.float32))[:, None] + 0.5 + noise


def block_scale(rng, extent, cuts, least, largest):
    gain, own = 1.0, jax.random.fold_in(rng, 6)
    for axis_at, blocks in cuts:
        draws = jnp.exp(jax.random.uniform(jax.random.fold_in(own, axis_at), (blocks,), jnp.float32, least / len(cuts), largest / len(cuts)))
        gain = gain * jnp.repeat(draws, extent[axis_at] // blocks).reshape([-1 if axis == axis_at else 1 for axis in range(len(extent))])
    return gain


def gaussian(own_key, extent, spread, limit, cuts=(), held_as=jnp.bfloat16):
    entries = spread * jax.random.normal(own_key, extent, jnp.float32)
    if cuts:
        entries = entries * block_scale(own_key, extent, cuts, -0.22, 0.18)
    return jnp.clip(entries, -limit, limit).astype(held_as)


def setup_inputs(seed: int = 0) -> dict:
    arg_keys = jax.random.split(jax.random.key(seed), 10)
    queries = gaussian(arg_keys[0], (TOKENS, HEADS * HEAD_DIM), 1.0, 6.0, ((0, 512),))
    grad_out = gaussian(arg_keys[1], (TOKENS, HEADS * HEAD_DIM), 1.0, 6.0, ((0, 512),))
    attn_out = gaussian(arg_keys[2], (TOKENS, HEADS * HEAD_DIM), 0.3, 2.0, ((0, 512),))
    key_states = gaussian(arg_keys[3], (TOKENS, HEAD_DIM), 1.0, 6.0, ((0, 512),))
    value_states = gaussian(arg_keys[4], (TOKENS, HEAD_DIM), 0.3, 2.0, ((0, 512),))
    log_norm = draw_log_norm(jax.random.fold_in(arg_keys[9], 71), 0)
    position = draw_position(jax.random.fold_in(arg_keys[9], 71), 0)
    modality = draw_modality(jax.random.fold_in(arg_keys[9], 71), 0)
    bidirectional = draw_bidirectional(jax.random.fold_in(arg_keys[9], 71), 0)
    return dict(queries=queries, grad_out=grad_out, attn_out=attn_out, key_states=key_states, value_states=value_states, log_norm=log_norm, position=position, modality=modality, bidirectional=bidirectional)


def split_seqs(array):
    tail = array.shape[1:]
    grid = array.reshape((N_ROW, SEQS, 2 * TOK_DEV) + tail)
    return jnp.moveaxis(grid, 1, 0).reshape((SEQS, SEQ_LEN) + tail)


def join_seqs(array):
    tail = array.shape[2:]
    grid = array.reshape((SEQS, N_ROW, 2 * TOK_DEV) + tail)
    return jnp.moveaxis(grid, 0, 1).reshape((TOKENS,) + tail)


def tile_grads(q_rows, d_rows, lse_rows, delta_rows, q_pos, q_mod, key_states, value_states, position, modality, table):
    row_count = q_rows.shape[0]
    flat_q = q_rows.reshape(row_count * HEADS, HEAD_DIM)
    flat_d = d_rows.reshape(row_count * HEADS, HEAD_DIM)
    score_scale = HEAD_DIM ** -0.5
    scores = jnp.dot(flat_q, key_states.T, preferred_element_type=jnp.float32) * score_scale
    causal = position[None, :] <= q_pos[:, None]
    same_unit = (position[None, :] // UNIT) == (q_pos[:, None] // UNIT)
    pair_bid = table[q_mod[:, None], modality[None, :]] == 1
    allowed = jnp.repeat(causal | (same_unit & pair_bid), HEADS, axis=0)
    attn_probs = jnp.where(allowed, jnp.exp(scores - lse_rows.reshape(-1, 1)), 0.0)
    probs_low = attn_probs.astype(jnp.bfloat16)
    grad_probs = jnp.dot(flat_d, value_states.T, preferred_element_type=jnp.float32)
    grad_scores = attn_probs * (grad_probs - delta_rows.reshape(-1, 1))
    scores_low = grad_scores.astype(jnp.bfloat16)
    grad_q = jnp.dot(scores_low, key_states, preferred_element_type=jnp.float32) * score_scale
    grad_k = jnp.dot(scores_low.T, flat_q, preferred_element_type=jnp.float32) * score_scale
    grad_v = jnp.dot(probs_low.T, flat_d, preferred_element_type=jnp.float32)
    return grad_q.reshape(row_count, HEADS * HEAD_DIM), grad_k, grad_v


def sequence_grads(table, pieces):
    queries, grad_out, row_delta, key_states, value_states, log_norm, position, modality = pieces
    block_len = math.gcd(SEQ_LEN, 512)

    def step_fn(totals, block_index):
        start = (block_index * block_len).astype(jnp.int32)
        q_rows = lax.dynamic_slice_in_dim(queries, start, block_len)
        d_rows = lax.dynamic_slice_in_dim(grad_out, start, block_len)
        lse_rows = lax.dynamic_slice_in_dim(log_norm, start, block_len)
        delta_rows = lax.dynamic_slice_in_dim(row_delta, start, block_len)
        q_pos = lax.dynamic_slice_in_dim(position, start, block_len)
        q_mod = lax.dynamic_slice_in_dim(modality, start, block_len)
        grad_q, grad_k, grad_v = tile_grads(q_rows, d_rows, lse_rows, delta_rows, q_pos, q_mod,
                                            key_states, value_states, position, modality, table)
        return (totals[0] + grad_k, totals[1] + grad_v), grad_q

    empty = jnp.zeros((SEQ_LEN, HEAD_DIM), jnp.float32)
    totals, grad_blocks = lax.scan(step_fn, (empty, empty), jnp.arange(SEQ_LEN // block_len, dtype=jnp.int32))
    return grad_blocks.reshape(SEQ_LEN, HEADS * HEAD_DIM), totals[0], totals[1]


def reference(queries, grad_out, attn_out, key_states, value_states, log_norm, position, modality, bidirectional):
    row_delta = jnp.einsum(
        "thd,thd->th",
        grad_out.astype(jnp.float32).reshape(TOKENS, HEADS, HEAD_DIM),
        attn_out.astype(jnp.float32).reshape(TOKENS, HEADS, HEAD_DIM),
    )
    pieces = tuple(split_seqs(array) for array in
                   (queries, grad_out, row_delta, key_states, value_states, log_norm, position, modality))
    grad_q, grad_k, grad_v = lax.map(functools.partial(sequence_grads, bidirectional), pieces)
    return (join_seqs(grad_q).astype(jnp.bfloat16), join_seqs(grad_k).astype(jnp.bfloat16),
            join_seqs(grad_v).astype(jnp.bfloat16))
```

```python
import functools
import jax
import jax.numpy as jnp
from jax import lax
from jax.experimental import pallas as pl
from jax.experimental.pallas import tpu as pltpu
from jax.sharding import Mesh, PartitionSpec as P

UNIT = 64
TOK = 128
HEADS = 4
DIM = 128
WIDE = HEADS * DIM
MSG = 2 * WIDE + DIM
NZ = 4
NY = 8
KEYS = 2 * NY * TOK
QUNITS = 2 * NZ
KUNITS = KEYS // UNIT
GROUP = 8
ROWS = HEADS * UNIT
AXES = ("y", "zlo", "core", "x", "zhh", "zhl")
bf16 = jnp.bfloat16
f32 = jnp.float32


def pack_kernel(q_ref, d_ref, o_ref, lse_ref, msg_ref):
    msg_ref[:, :WIDE] = q_ref[...]
    msg_ref[:, WIDE : 2 * WIDE] = d_ref[...]
    lane = lax.broadcasted_iota(jnp.int32, (TOK, DIM), 1)
    extra = jnp.zeros((TOK, DIM), f32)
    for h in range(HEADS):
        cut = slice(h * DIM, (h + 1) * DIM)
        delta = jnp.sum(d_ref[:, cut].astype(f32) * o_ref[:, cut].astype(f32), axis=1, keepdims=True)
        for base, col in ((h, lse_ref[:, h : h + 1]), (3 * HEADS + h, delta)):
            rest = jnp.broadcast_to(col, (TOK, DIM))
            for part in range(3):
                low = rest.astype(bf16).astype(f32)
                extra = jnp.where(lane == base + part * HEADS, low, extra)
                rest = rest - low
    msg_ref[:, 2 * WIDE :] = extra.astype(bf16)


def nt(left, right):
    return lax.dot_general(left, right, (((1,), (1,)), ((), ())), preferred_element_type=f32)


def tn(left, right):
    return lax.dot_general(left, right, (((0,), (0,)), ((), ())), preferred_element_type=f32)


def nn(left, right):
    return lax.dot_general(left, right, (((1,), (0,)), ((), ())), preferred_element_type=f32)


def tile_kernel(
    order, need, full, m0, m1, m2, m3, kvo, kvx, kcode, qlim,
    g0, g1, g2, g3, gkvo, gkvx,
    qs, ds, lse, delta, kv, kc, gk, gv, gq,
):
    for a, m in enumerate((m0, m1, m2, m3)):
        meta = m[:, 2 * WIDE :].astype(f32).T
        for half in range(2):
            u = 2 * a + half
            rows = slice(half * UNIT, (half + 1) * UNIT)
            for h in range(HEADS):
                dst = slice(u * ROWS + h * UNIT, u * ROWS + (h + 1) * UNIT)
                qs[dst, :] = m[rows, h * DIM : (h + 1) * DIM]
                ds[dst, :] = m[rows, WIDE + h * DIM : WIDE + (h + 1) * DIM]
            for ref, base in ((lse, 0), (delta, 3 * HEADS)):
                ref[u] = jnp.concatenate(
                    [
                        meta[base + h : base + h + 1, rows]
                        + meta[base + HEADS + h : base + HEADS + h + 1, rows]
                        + meta[base + 2 * HEADS + h : base + 2 * HEADS + h + 1, rows]
                        for h in range(HEADS)
                    ],
                    axis=1,
                )
    half_keys = KEYS // 2
    kv[:half_keys, :] = kvo[...]
    kv[half_keys:, :] = kvx[...]
    for b in range(2 * NY):
        kc[b * TOK : (b + 1) * TOK, :] = jnp.broadcast_to(kcode[b : b + 1, :], (TOK, TOK)).T
    gk[...] = jnp.zeros_like(gk)
    gv[...] = jnp.zeros_like(gv)
    gq[...] = jnp.zeros_like(gq)
    score_scale = DIM ** (-0.5)

    def step(u, c, masked):
        offs = [pl.multiple_of(order[c * GROUP + i] * UNIT, UNIT) for i in range(GROUP)]
        keys = jnp.concatenate([kv[pl.ds(o, UNIT), :DIM] for o in offs], axis=0)
        vals = jnp.concatenate([kv[pl.ds(o, UNIT), DIM:] for o in offs], axis=0)
        at = pl.multiple_of(u * ROWS, ROWS)
        q = qs[pl.ds(at, ROWS), :]
        d = ds[pl.ds(at, ROWS), :]
        probs = jnp.exp(nt(keys, q) * score_scale - lse[u])
        if masked:
            code = jnp.concatenate([kc[pl.ds(o, UNIT), :] for o in offs], axis=0)
            code = jnp.concatenate([code] * (ROWS // TOK), axis=1)
            mod = code & 3
            lim = qlim[u]
            bound = jnp.where(mod == 0, lim[0:1], jnp.where(mod == 1, lim[1:2], lim[2:3]))
            probs = jnp.where((code >> 2) <= bound, probs, 0.0)
        grads = probs * (nt(vals, d) - delta[u])
        plow = probs.astype(bf16)
        glow = grads.astype(bf16)
        pv = nn(plow, d)
        pk = nn(glow, q)
        for i, o in enumerate(offs):
            gv[pl.ds(o, UNIT), :] += pv[i * UNIT : (i + 1) * UNIT]
            gk[pl.ds(o, UNIT), :] += pk[i * UNIT : (i + 1) * UNIT]
        gq[u] += tn(glow, keys)

    def unit(u, _):
        plain = full[u] // GROUP
        last = (need[u] + GROUP - 1) // GROUP

        def plain_step(c, _):
            step(u, c, False)
            return 0

        def masked_step(c, _):
            step(u, c, True)
            return 0

        lax.fori_loop(0, plain, plain_step, 0)
        lax.fori_loop(plain, last, masked_step, 0)
        return 0

    lax.fori_loop(0, QUNITS, unit, 0)
    for a, g in enumerate((g0, g1, g2, g3)):
        for half in range(2):
            rows = slice(half * UNIT, (half + 1) * UNIT)
            for h in range(HEADS):
                part = gq[2 * a + half, h * UNIT : (h + 1) * UNIT, :]
                g[rows, h * DIM : (h + 1) * DIM] = part.astype(g.dtype)
    gkvo[:, :DIM] = gk[:half_keys, :]
    gkvo[:, DIM:] = gv[:half_keys, :]
    gkvx[:, :DIM] = gk[half_keys:, :].astype(bf16)
    gkvx[:, DIM:] = gv[half_keys:, :].astype(bf16)


def plan(position, modality, table):
    code = (position * 4 + modality).reshape(8, 2, 2, 4, 2, 2, TOK)
    y, zlo, core, x, zhh, zhl = (lax.axis_index(a) for a in AXES)
    kcode = lax.dynamic_slice(code, (0, zlo, 0, x, zhh, zhl, 0), (8, 1, 2, 1, 1, 1, TOK))
    kcode = kcode.reshape(8, 2, TOK)
    kcode = jnp.where(core == 0, jnp.stack([kcode[:, 0], kcode[:, 1]]), jnp.stack([kcode[:, 1], kcode[:, 0]]))
    qcode = lax.dynamic_slice(code, (y, 0, core, x, zhh, 0, 0), (1, 2, 1, 1, 1, 2, TOK)).reshape(4, TOK)
    own = zlo * 2 + zhl
    pick = (own ^ jnp.arange(4))[:, None, None] == jnp.arange(4)[None, :, None]
    qcode = jnp.sum(jnp.where(pick, qcode[None], 0), axis=1)
    qpos, qmod = (qcode >> 2).reshape(QUNITS, UNIT), (qcode & 3).reshape(QUNITS, UNIT)
    bids = [
        jnp.where(qmod == 0, table[0, m], jnp.where(qmod == 1, table[1, m], table[2, m])) for m in range(3)
    ]
    lim = jnp.stack([jnp.where(b == 1, qpos | (UNIT - 1), qpos) for b in bids], axis=1)
    qlim = jnp.concatenate([lim] * HEADS, axis=2)
    kunit = (kcode >> 2).reshape(KUNITS, UNIT)
    low, high = jnp.min(kunit, axis=1), jnp.max(kunit, axis=1)
    index = jnp.arange(KUNITS)
    before = (low[None, :] < low[:, None]) | ((low[None, :] == low[:, None]) & (index[None, :] < index[:, None]))
    rank = jnp.sum(before.astype(jnp.int32), axis=1)
    order = jnp.sum(jnp.where(rank[None, :] == index[:, None], index[None, :], 0), axis=1)
    qlow, qhigh = jnp.min(qpos, axis=1), jnp.max(qpos, axis=1)
    need = jnp.sum((low[None, :] // UNIT <= qhigh[:, None] // UNIT).astype(jnp.int32), axis=1)
    full = jnp.min(jnp.where(high[None, :] > qlow[:, None], rank[None, :], KUNITS), axis=1)
    return order, need, full, kcode.reshape(2 * NY, TOK), qlim


def shards(queries, grad_out, attn_out, key_states, value_states, log_norm, position, modality, table):
    msg = pl.pallas_call(
        pack_kernel, out_shape=jax.ShapeDtypeStruct((TOK, MSG), bf16), name="pack"
    )(queries, grad_out, attn_out, log_norm)

    def along_z(value, mask):
        return lax.ppermute(value, ("zlo", "zhl"), [(i, i ^ mask) for i in range(NZ)])

    def other_core(value):
        return lax.ppermute(value, "core", [(0, 1), (1, 0)])

    def over_y(value):
        return lax.all_to_all(value, "y", 0, 0)

    msgs = [along_z(msg, mask) for mask in (1, 2, 3)]
    pair = jnp.concatenate([key_states, value_states], axis=1)
    kvo = over_y(jnp.broadcast_to(pair[None], (NY, TOK, 2 * DIM))).reshape(NY * TOK, 2 * DIM)
    kvx = other_core(kvo)
    order, need, full, kcode, qlim = plan(position, modality, table)
    smem = pl.BlockSpec(memory_space=pltpu.SMEM)
    vmem = pl.BlockSpec(memory_space=pltpu.VMEM)
    part = jax.ShapeDtypeStruct((TOK, WIDE), bf16)
    g0, g1, g2, g3, gkvo, gkvx = pl.pallas_call(
        tile_kernel,
        in_specs=[smem] * 3 + [vmem] * 8,
        out_specs=[vmem] * 6,
        out_shape=[
            jax.ShapeDtypeStruct((TOK, WIDE), f32),
            part,
            part,
            part,
            jax.ShapeDtypeStruct((NY * TOK, 2 * DIM), f32),
            jax.ShapeDtypeStruct((NY * TOK, 2 * DIM), bf16),
        ],
        scratch_shapes=[
            pltpu.VMEM((QUNITS * ROWS, DIM), bf16),
            pltpu.VMEM((QUNITS * ROWS, DIM), bf16),
            pltpu.VMEM((QUNITS, 1, ROWS), f32),
            pltpu.VMEM((QUNITS, 1, ROWS), f32),
            pltpu.VMEM((KEYS, 2 * DIM), bf16),
            pltpu.VMEM((KEYS, DIM), jnp.int32),
            pltpu.VMEM((KEYS, DIM), f32),
            pltpu.VMEM((KEYS, DIM), f32),
            pltpu.VMEM((QUNITS, ROWS, DIM), f32),
        ],
        name="tile",
    )(order, need, full, msg, *msgs, kvo, kvx, kcode, qlim)
    got = other_core(gkvx)
    back = [along_z(g, mask) for g, mask in ((g1, 1), (g2, 2), (g3, 3))]
    paired = (gkvo + got.astype(f32)).astype(bf16).reshape(NY, TOK, 2 * DIM)
    summed = jnp.sum(over_y(paired).astype(f32), axis=0)
    score_scale = DIM ** (-0.5)
    grad_q = (g0 + back[0].astype(f32) + back[1].astype(f32) + back[2].astype(f32)) * score_scale
    return (
        grad_q.astype(bf16),
        (summed[:, :DIM] * score_scale).astype(bf16),
        summed[:, DIM:].astype(bf16),
    )


def solution(mesh):
    fine = Mesh(mesh.devices.reshape(8, 2, 2, 4, 2, 2), AXES)
    tokens = P(AXES, None)
    return jax.shard_map(
        shards,
        mesh=fine,
        in_specs=(tokens,) * 6 + (P(), P(), P()),
        out_specs=(tokens,) * 3,
        check_vma=False,
    )
```

```python
import jax
import jax.numpy as jnp
from jax import lax
from jax.experimental import pallas as pl
from jax.experimental.pallas import tpu as pltpu
from jax.sharding import Mesh, PartitionSpec as P

UNIT = 64
TOK = 128
HEADS = 4
DIM = 128
WIDE = HEADS * DIM
MSG = 2 * WIDE + DIM
NZ = 4
NY = 8
KEYS = 2 * NY * TOK
QUNITS = 2 * NZ
KUNITS = KEYS // UNIT
GROUP = 8
ROWS = HEADS * UNIT
AXES = ("y", "zlo", "core", "x", "zhh", "zhl")
bf16 = jnp.bfloat16
f32 = jnp.float32


def pack_kernel(q_ref, d_ref, o_ref, lse_ref, msg_ref):
    msg_ref[:, :WIDE] = q_ref[...]
    msg_ref[:, WIDE : 2 * WIDE] = d_ref[...]
    lane = lax.broadcasted_iota(jnp.int32, (TOK, DIM), 1)
    delta = jnp.zeros((TOK, DIM), f32)
    for h in range(HEADS):
        cut = slice(h * DIM, (h + 1) * DIM)
        column = jnp.sum(d_ref[:, cut].astype(f32) * o_ref[:, cut].astype(f32), axis=1, keepdims=True)
        delta = jnp.where(lane == h, column, delta)
    rest = jnp.concatenate([lse_ref[...], delta.T[:HEADS]], axis=0)
    parts = []
    for _ in range(3):
        low = rest.astype(bf16).astype(f32)
        parts.append(low)
        rest = rest - low
    parts.append(jnp.zeros((TOK - 6 * HEADS, DIM), f32))
    msg_ref[:, 2 * WIDE :] = jnp.concatenate(parts, axis=0).astype(bf16)


def nt(left, right):
    return lax.dot_general(left, right, (((1,), (1,)), ((), ())), preferred_element_type=f32)


def tn(left, right):
    return lax.dot_general(left, right, (((0,), (0,)), ((), ())), preferred_element_type=f32)


def nn(left, right):
    return lax.dot_general(left, right, (((1,), (0,)), ((), ())), preferred_element_type=f32)


def tile_kernel(
    order, need, full, m0, m1, m2, m3, kvo, kvx, kcode, qlim,
    g0, g1, g2, g3, gkvo, gkvx,
    qs, ds, lse, delta, kv, kc, gk, gv, gq,
):
    for a, m in enumerate((m0, m1, m2, m3)):
        meta = m[: 8 * HEADS, 2 * WIDE :].astype(f32)
        meta = meta[: 2 * HEADS] + meta[2 * HEADS : 4 * HEADS] + meta[4 * HEADS : 6 * HEADS]
        for half in range(2):
            u = 2 * a + half
            rows = slice(half * UNIT, (half + 1) * UNIT)
            for h in range(HEADS):
                dst = slice(u * ROWS + h * UNIT, u * ROWS + (h + 1) * UNIT)
                qs[dst, :] = m[rows, h * DIM : (h + 1) * DIM]
                ds[dst, :] = m[rows, WIDE + h * DIM : WIDE + (h + 1) * DIM]
            for ref, base in ((lse, 0), (delta, HEADS)):
                ref[u] = jnp.concatenate([meta[base + h : base + h + 1, rows] for h in range(HEADS)], axis=1)
    half_keys = KEYS // 2
    kv[:half_keys, :] = kvo[...]
    kv[half_keys:, :] = kvx[...]
    for b in range(2 * NY):
        kc[b * TOK : (b + 1) * TOK, :] = jnp.broadcast_to(kcode[b : b + 1, :], (TOK, TOK)).T
    gk[...] = jnp.zeros_like(gk)
    gv[...] = jnp.zeros_like(gv)
    gq[...] = jnp.zeros_like(gq)
    score_scale = DIM ** (-0.5)

    def step(u, c, masked):
        offs = [pl.multiple_of(order[c * GROUP + i] * UNIT, UNIT) for i in range(GROUP)]
        keys = jnp.concatenate([kv[pl.ds(o, UNIT), :DIM] for o in offs], axis=0)
        vals = jnp.concatenate([kv[pl.ds(o, UNIT), DIM:] for o in offs], axis=0)
        at = pl.multiple_of(u * ROWS, ROWS)
        q = qs[pl.ds(at, ROWS), :]
        d = ds[pl.ds(at, ROWS), :]
        probs = jnp.exp(nt(keys, q) * score_scale - lse[u])
        if masked:
            code = jnp.concatenate([kc[pl.ds(o, UNIT), :] for o in offs], axis=0)
            code = jnp.concatenate([code] * (ROWS // TOK), axis=1)
            mod = code & 3
            lim = qlim[u]
            bound = jnp.where(mod == 0, lim[0:1], jnp.where(mod == 1, lim[1:2], lim[2:3]))
            probs = jnp.where((code >> 2) <= bound, probs, 0.0)
        grads = probs * (nt(vals, d) - delta[u])
        plow = probs.astype(bf16)
        glow = grads.astype(bf16)
        pv = nn(plow, d)
        pk = nn(glow, q)
        for i, o in enumerate(offs):
            gv[pl.ds(o, UNIT), :] += pv[i * UNIT : (i + 1) * UNIT]
            gk[pl.ds(o, UNIT), :] += pk[i * UNIT : (i + 1) * UNIT]
        gq[u] += tn(glow, keys)

    def unit(u, _):
        plain = full[u] // GROUP
        last = (need[u] + GROUP - 1) // GROUP

        def plain_step(c, _):
            step(u, c, False)
            return 0

        def masked_step(c, _):
            step(u, c, True)
            return 0

        lax.fori_loop(0, plain, plain_step, 0)
        lax.fori_loop(plain, last, masked_step, 0)
        return 0

    lax.fori_loop(0, QUNITS, unit, 0)
    for a, g in enumerate((g0, g1, g2, g3)):
        for half in range(2):
            rows = slice(half * UNIT, (half + 1) * UNIT)
            for h in range(HEADS):
                part = gq[2 * a + half, h * UNIT : (h + 1) * UNIT, :]
                g[rows, h * DIM : (h + 1) * DIM] = part.astype(g.dtype)
    gkvo[:, :DIM] = gk[:half_keys, :]
    gkvo[:, DIM:] = gv[:half_keys, :]
    gkvx[:, :DIM] = gk[half_keys:, :].astype(bf16)
    gkvx[:, DIM:] = gv[half_keys:, :].astype(bf16)


def plan(position, modality, table):
    code = (position * 4 + modality).reshape(8, 2, 2, 4, 2, 2, TOK)
    y, zlo, core, x, zhh, zhl = (lax.axis_index(a) for a in AXES)
    kcode = lax.dynamic_slice(code, (0, zlo, 0, x, zhh, zhl, 0), (8, 1, 2, 1, 1, 1, TOK))
    kcode = kcode.reshape(8, 2, TOK)
    kcode = jnp.where(core == 0, jnp.stack([kcode[:, 0], kcode[:, 1]]), jnp.stack([kcode[:, 1], kcode[:, 0]]))
    qcode = lax.dynamic_slice(code, (y, 0, core, x, zhh, 0, 0), (1, 2, 1, 1, 1, 2, TOK)).reshape(4, TOK)
    own = zlo * 2 + zhl
    pick = (own ^ jnp.arange(4))[:, None, None] == jnp.arange(4)[None, :, None]
    qcode = jnp.sum(jnp.where(pick, qcode[None], 0), axis=1)
    qpos, qmod = (qcode >> 2).reshape(QUNITS, UNIT), (qcode & 3).reshape(QUNITS, UNIT)
    bids = [
        jnp.where(qmod == 0, table[0, m], jnp.where(qmod == 1, table[1, m], table[2, m])) for m in range(3)
    ]
    lim = jnp.stack([jnp.where(b == 1, qpos | (UNIT - 1), qpos) for b in bids], axis=1)
    qlim = jnp.concatenate([lim] * HEADS, axis=2)
    kunit = (kcode >> 2).reshape(KUNITS, UNIT)
    low, high = jnp.min(kunit, axis=1), jnp.max(kunit, axis=1)
    index = jnp.arange(KUNITS)
    before = (low[None, :] < low[:, None]) | ((low[None, :] == low[:, None]) & (index[None, :] < index[:, None]))
    rank = jnp.sum(before.astype(jnp.int32), axis=1)
    order = jnp.sum(jnp.where(rank[None, :] == index[:, None], index[None, :], 0), axis=1)
    qlow, qhigh = jnp.min(qpos, axis=1), jnp.max(qpos, axis=1)
    need = jnp.sum((low[None, :] // UNIT <= qhigh[:, None] // UNIT).astype(jnp.int32), axis=1)
    full = jnp.min(jnp.where(high[None, :] > qlow[:, None], rank[None, :], KUNITS), axis=1)
    return order, need, full, kcode.reshape(2 * NY, TOK), qlim


def shards(queries, grad_out, attn_out, key_states, value_states, log_norm, position, modality, table):
    def along_z(value, mask):
        return lax.ppermute(value, ("zlo", "zhl"), [(i, i ^ mask) for i in range(NZ)])

    def other_core(value):
        return lax.ppermute(value, "core", [(0, 1), (1, 0)])

    def over_y(value):
        return lax.all_to_all(value, "y", 0, 0)

    pair = jnp.concatenate([key_states, value_states], axis=1)
    copies = jnp.broadcast_to(pair[None], (NY, TOK, 2 * DIM))
    copies, queries = lax.optimization_barrier((copies, queries))
    msg = pl.pallas_call(
        pack_kernel, out_shape=pltpu.VMEM((TOK, MSG), bf16), compiler_params=pltpu.CompilerParams(vmem_limit_bytes=8 << 20), name="pack"
    )(queries, grad_out, attn_out, log_norm.T)
    kvo = over_y(copies).reshape(NY * TOK, 2 * DIM)
    msgs = [along_z(msg, mask) for mask in (1, 2, 3)]
    kvx = other_core(kvo)
    order, need, full, kcode, qlim = plan(position, modality, table)
    smem = pl.BlockSpec(memory_space=pltpu.SMEM)
    vmem = pl.BlockSpec(memory_space=pltpu.VMEM)
    part = pltpu.VMEM((TOK, WIDE), bf16)
    g0, g1, g2, g3, gkvo, gkvx = pl.pallas_call(
        tile_kernel,
        in_specs=[smem] * 3 + [vmem] * 8,
        out_specs=[vmem] * 6,
        out_shape=[
            pltpu.VMEM((TOK, WIDE), f32),
            part,
            part,
            part,
            pltpu.VMEM((NY * TOK, 2 * DIM), f32),
            pltpu.VMEM((NY * TOK, 2 * DIM), bf16),
        ],
        scratch_shapes=[
            pltpu.VMEM((QUNITS * ROWS, DIM), bf16),
            pltpu.VMEM((QUNITS * ROWS, DIM), bf16),
            pltpu.VMEM((QUNITS, 1, ROWS), f32),
            pltpu.VMEM((QUNITS, 1, ROWS), f32),
            pltpu.VMEM((KEYS, 2 * DIM), bf16),
            pltpu.VMEM((KEYS, DIM), jnp.int32),
            pltpu.VMEM((KEYS, DIM), f32),
            pltpu.VMEM((KEYS, DIM), f32),
            pltpu.VMEM((QUNITS, ROWS, DIM), f32),
        ],
        compiler_params=pltpu.CompilerParams(vmem_limit_bytes=28 << 20),
        name="tile",
    )(order, need, full, *[pltpu.with_memory_space_constraint(v, pltpu.VMEM) for v in (msg, *msgs, kvo, kvx, kcode, qlim)])
    got = other_core(gkvx)
    back = [along_z(g, mask) for g, mask in ((g1, 1), (g2, 2), (g3, 3))]
    paired = (gkvo + got.astype(f32)).astype(bf16).reshape(NY, TOK, 2 * DIM)
    summed = jnp.sum(over_y(paired).astype(f32), axis=0)
    score_scale = DIM ** (-0.5)
    grad_q = (g0 + back[0].astype(f32) + back[1].astype(f32) + back[2].astype(f32)) * score_scale
    return (
        grad_q.astype(bf16),
        (summed[:, :DIM] * score_scale).astype(bf16),
        summed[:, DIM:].astype(bf16),
    )


def solution(mesh):
    fine = Mesh(mesh.devices.reshape(8, 2, 2, 4, 2, 2), AXES)
    tokens = P(AXES, None)

    return jax.shard_map(
        shards,
        mesh=fine,
        in_specs=(tokens,) * 6 + (P(), P(), P()),
        out_specs=(tokens,) * 3,
        check_vma=False,
    )
```

```python
import jax
import jax.numpy as jnp
from jax import lax
from jax.experimental import pallas as pl
from jax.experimental.pallas import tpu as pltpu
from jax.sharding import Mesh, PartitionSpec as P

UNIT = 64
TOK = 128
HEADS = 4
DIM = 128
WIDE = HEADS * DIM
NZ = 4
NY = 8
QUNITS = 2 * NZ
KUNITS = NY * TOK // UNIT
GROUP = 8
MASKS = (0, 2, 1, 3)
ROWS = HEADS * UNIT
AXES = ("y", "zlo", "core", "x", "zhh", "zhl")
bf16 = jnp.bfloat16
f32 = jnp.float32


def pack_kernel(q_ref, d_ref, o_ref, lse_ref, msg_ref):
    msg_ref[:TOK, :WIDE] = q_ref[...]
    msg_ref[:TOK, WIDE:] = d_ref[...]
    lane = lax.broadcasted_iota(jnp.int32, (TOK, DIM), 1)
    delta = jnp.zeros((TOK, DIM), f32)
    for h in range(HEADS):
        cut = slice(h * DIM, (h + 1) * DIM)
        column = jnp.sum(d_ref[:, cut].astype(f32) * o_ref[:, cut].astype(f32), axis=1, keepdims=True)
        delta = jnp.where(lane == h, column, delta)
    delta = delta.T
    line = [lse_ref[h : h + 1, :] for h in range(HEADS)] + [delta[h : h + 1, :] for h in range(HEADS)]
    rest = jnp.concatenate(line, axis=1)
    parts = []
    for _ in range(3):
        low = rest.astype(bf16).astype(f32)
        parts.append(low)
        rest = rest - low
    parts.append(jnp.zeros((5, 2 * WIDE), f32))
    msg_ref[TOK:, :] = jnp.concatenate(parts, axis=0).astype(bf16)


def nt(left, right):
    return lax.dot_general(left, right, (((1,), (1,)), ((), ())), preferred_element_type=f32)


def tn(left, right):
    return lax.dot_general(left, right, (((0,), (0,)), ((), ())), preferred_element_type=f32)


def nn(left, right):
    return lax.dot_general(left, right, (((1,), (0,)), ((), ())), preferred_element_type=f32)


def tile_kernel(count, sets, chained, *refs):
    it = iter(refs)

    def take(n):
        return [next(it) for _ in range(n)]

    order, need, full = take(3)
    msgs = take(count)
    kvs = take(len(sets))
    kcode, qlim = take(2)
    olds = take(len(sets)) if chained is not None else []
    oldq = next(it) if chained == "last" else None
    gqs = take(1 if chained == "first" else count)
    gkvs = take(len(sets))
    qs, ds, lse, delta, kc, gk, gv, gq = it
    base = 0 if chained is None else QUNITS - 2 * count
    for a, m in enumerate(msgs):
        meta = m[TOK : TOK + 8].astype(f32)
        meta = meta[0:1] + meta[1:2] + meta[2:3]
        for half in range(2):
            u = 2 * a + half
            rows = slice(half * UNIT, (half + 1) * UNIT)
            for h in range(HEADS):
                dst = slice(u * ROWS + h * UNIT, u * ROWS + (h + 1) * UNIT)
                qs[dst, :] = m[rows, h * DIM : (h + 1) * DIM]
                ds[dst, :] = m[rows, WIDE + h * DIM : WIDE + (h + 1) * DIM]
            for ref, first in ((lse, 0), (delta, WIDE)):
                cuts = [first + h * TOK + half * UNIT for h in range(HEADS)]
                ref[u] = jnp.concatenate([meta[:, c : c + UNIT] for c in cuts], axis=1)
    gq[...] = jnp.zeros_like(gq) if oldq is None else oldq[...]
    score_scale = DIM ** (-0.5)
    for which, s in enumerate(sets):
        kv = kvs[which]
        for b in range(NY):
            row = kcode[s * NY + b : s * NY + b + 1, :]
            kc[b * TOK : (b + 1) * TOK, :] = jnp.broadcast_to(row, (TOK, TOK)).T
        if chained is None:
            gk[...] = jnp.zeros_like(gk)
            gv[...] = jnp.zeros_like(gv)
        else:
            gk[...] = olds[which][:, :DIM]
            gv[...] = olds[which][:, DIM:]

        def step(u, c, masked, s=s, kv=kv):
            offs = [pl.multiple_of(order[s * KUNITS + c * GROUP + i] * UNIT, UNIT) for i in range(GROUP)]
            keys = jnp.concatenate([kv[pl.ds(o, UNIT), :DIM] for o in offs], axis=0)
            vals = jnp.concatenate([kv[pl.ds(o, UNIT), DIM:] for o in offs], axis=0)
            at = pl.multiple_of(u * ROWS, ROWS)
            q = qs[pl.ds(at, ROWS), :]
            d = ds[pl.ds(at, ROWS), :]
            probs = jnp.exp(nt(keys, q) * score_scale - lse[u])
            if masked:
                code = jnp.concatenate([kc[pl.ds(o, UNIT), :] for o in offs], axis=0)
                code = jnp.concatenate([code] * (ROWS // TOK), axis=1)
                mod = code & 3
                lim = qlim[base + u]
                bound = jnp.where(mod == 0, lim[0:1], jnp.where(mod == 1, lim[1:2], lim[2:3]))
                probs = jnp.where((code >> 2) <= bound, probs, 0.0)
            grads = probs * (nt(vals, d) - delta[u])
            plow = probs.astype(bf16)
            glow = grads.astype(bf16)
            pv = nn(plow, d)
            pk = nn(glow, q)
            for i, o in enumerate(offs):
                gv[pl.ds(o, UNIT), :] += pv[i * UNIT : (i + 1) * UNIT]
                gk[pl.ds(o, UNIT), :] += pk[i * UNIT : (i + 1) * UNIT]
            gq[u] += tn(glow, keys)

        def unit(u, _, s=s, step=step):
            plain = full[s * QUNITS + base + u] // GROUP
            last = (need[s * QUNITS + base + u] + GROUP - 1) // GROUP

            def plain_step(c, _):
                step(u, c, False)
                return 0

            def masked_step(c, _):
                step(u, c, True)
                return 0

            lax.fori_loop(0, plain, plain_step, 0)
            lax.fori_loop(plain, last, masked_step, 0)
            return 0

        lax.fori_loop(0, 2 * count, unit, 0)
        out = gkvs[which]
        out[:, :DIM] = gk[...].astype(out.dtype)
        out[:, DIM:] = gv[...].astype(out.dtype)
    if chained == "first":
        gqs[0][...] = gq[...]
        return
    for a, g in enumerate(gqs):
        for half in range(2):
            rows = slice(half * UNIT, (half + 1) * UNIT)
            for h in range(HEADS):
                part = gq[2 * a + half, h * UNIT : (h + 1) * UNIT, :]
                g[rows, h * DIM : (h + 1) * DIM] = part.astype(g.dtype)


def in_vmem(value):
    return pltpu.with_memory_space_constraint(value, pltpu.VMEM)


def tile(tables, msgs, kvs, kcode, qlim, sets, chained=None, olds=(), oldq=None, gq_types=(), gkv_types=()):
    count = len(msgs)
    smem = pl.BlockSpec(memory_space=pltpu.SMEM)
    vmem = pl.BlockSpec(memory_space=pltpu.VMEM)
    arrays = [*msgs, *kvs, kcode, qlim, *olds] + ([] if oldq is None else [oldq])
    raw = pltpu.VMEM((2 * count, ROWS, DIM), f32)
    outs = [raw] if chained == "first" else [pltpu.VMEM((TOK, WIDE), t) for t in gq_types]
    outs += [pltpu.VMEM((NY * TOK, 2 * DIM), t) for t in gkv_types]

    def body(*refs):
        tile_kernel(count, sets, chained, *refs)

    return pl.pallas_call(
        body,
        in_specs=[smem] * 3 + [vmem] * len(arrays),
        out_specs=[vmem] * len(outs),
        out_shape=outs,
        scratch_shapes=[
            pltpu.VMEM((2 * count * ROWS, DIM), bf16),
            pltpu.VMEM((2 * count * ROWS, DIM), bf16),
            pltpu.VMEM((2 * count, 1, ROWS), f32),
            pltpu.VMEM((2 * count, 1, ROWS), f32),
            pltpu.VMEM((NY * TOK, DIM), jnp.int32),
            pltpu.VMEM((NY * TOK, DIM), f32),
            pltpu.VMEM((NY * TOK, DIM), f32),
            pltpu.VMEM((2 * count, ROWS, DIM), f32),
        ],
        compiler_params=pltpu.CompilerParams(vmem_limit_bytes=20 << 20),
    )(*tables, *[in_vmem(v) for v in arrays])


def plan(position, modality, table):
    code = (position * 4 + modality).reshape(8, 2, 2, 4, 2, 2, TOK)
    y, zlo, core, x, zhh, zhl = (lax.axis_index(a) for a in AXES)
    kcode = lax.dynamic_slice(code, (0, zlo, 0, x, zhh, zhl, 0), (8, 1, 2, 1, 1, 1, TOK))
    kcode = kcode.reshape(8, 2, TOK)
    kcode = jnp.where(core == 0, jnp.stack([kcode[:, 0], kcode[:, 1]]), jnp.stack([kcode[:, 1], kcode[:, 0]]))
    qcode = lax.dynamic_slice(code, (y, 0, core, x, zhh, 0, 0), (1, 2, 1, 1, 1, 2, TOK)).reshape(4, TOK)
    return tables_of(kcode, qcode, zlo * 2 + zhl, table)


def tables_of(kcode, qcode, own, table):
    masks = jnp.array(MASKS)
    pick = (own ^ masks)[:, None, None] == jnp.arange(4)[None, :, None]
    qcode = jnp.sum(jnp.where(pick, qcode[None], 0), axis=1)
    qpos, qmod = (qcode >> 2).reshape(QUNITS, UNIT), (qcode & 3).reshape(QUNITS, UNIT)
    bids = [
        jnp.where(qmod == 0, table[0, m], jnp.where(qmod == 1, table[1, m], table[2, m])) for m in range(3)
    ]
    lim = jnp.stack([jnp.where(b == 1, qpos | (UNIT - 1), qpos) for b in bids], axis=1)
    qlim = jnp.concatenate([lim] * HEADS, axis=2)
    kunit = (kcode >> 2).reshape(2, KUNITS, UNIT)
    low, high = jnp.min(kunit, axis=2), jnp.max(kunit, axis=2)
    index = jnp.arange(KUNITS)
    a, b = low[:, None, :], low[:, :, None]
    before = (a < b) | ((a == b) & (index[None, None, :] < index[None, :, None]))
    rank = jnp.sum(before.astype(jnp.int32), axis=2)
    order = jnp.sum(jnp.where(rank[:, None, :] == index[None, :, None], index[None, None, :], 0), axis=2)
    qlow, qhigh = jnp.min(qpos, axis=1), jnp.max(qpos, axis=1)
    need = jnp.sum((a // UNIT <= qhigh[None, :, None] // UNIT).astype(jnp.int32), axis=2)
    full = jnp.min(jnp.where(high[:, None, :] > qlow[None, :, None], rank[:, None, :], KUNITS), axis=2)
    return (order.reshape(-1), need.reshape(-1), full.reshape(-1)), kcode.reshape(2 * NY, TOK), qlim


def shards(queries, grad_out, attn_out, key_states, value_states, log_norm, position, modality, table):
    def along_z(value, mask):
        return lax.ppermute(value, ("zlo", "zhl"), [(i, i ^ mask) for i in range(NZ)])

    def other_core(value):
        return lax.ppermute(value, "core", [(0, 1), (1, 0)])

    def over_y(value):
        return lax.all_to_all(value, "y", 0, 0)

    pair = jnp.concatenate([key_states, value_states], axis=1)
    copies = jnp.broadcast_to(pair[None], (NY, TOK, 2 * DIM))
    copies, queries = lax.optimization_barrier((copies, queries))
    msg = pl.pallas_call(
        pack_kernel, out_shape=pltpu.VMEM((TOK + 8, 2 * WIDE), bf16), compiler_params=pltpu.CompilerParams(vmem_limit_bytes=8 << 20), name="pack"
    )(queries, grad_out, attn_out, log_norm.T)
    kvo = over_y(copies).reshape(NY * TOK, 2 * DIM)
    near = along_z(msg, MASKS[1])
    far, last = along_z(msg, MASKS[2]), along_z(msg, MASKS[3])
    kvx = other_core(kvo)
    tables, kcode, qlim = plan(position, modality, table)
    own_q, near_q, old_own, old_oth = tile(
        tables, (msg, near), (kvo, kvx), kcode, qlim, (0, 1), gq_types=(f32, bf16), gkv_types=(f32, f32)
    )
    raw_q, gkvx = tile(
        tables, (far, last), (kvx,), kcode, qlim, (1,), "first", (old_oth,), gkv_types=(bf16,)
    )
    got = other_core(gkvx)
    far_q, last_q, gkvo = tile(
        tables, (far, last), (kvo,), kcode, qlim, (0,), "last", (old_own,), raw_q, (bf16, bf16), (f32,)
    )
    paired = (gkvo + got.astype(f32)).astype(bf16).reshape(NY, TOK, 2 * DIM)
    summed = jnp.sum(over_y(paired).astype(f32), axis=0)
    back = [along_z(near_q, MASKS[1])]
    back += [along_z(far_q, MASKS[2]), along_z(last_q, MASKS[3])]
    g0 = own_q
    score_scale = DIM ** (-0.5)
    grad_q = (g0 + back[0].astype(f32) + back[1].astype(f32) + back[2].astype(f32)) * score_scale
    return (
        grad_q.astype(bf16),
        (summed[:, :DIM] * score_scale).astype(bf16),
        summed[:, DIM:].astype(bf16),
    )


def solution(mesh):
    fine = Mesh(mesh.devices.reshape(8, 2, 2, 4, 2, 2), AXES)
    tokens = P(AXES, None)

    return jax.shard_map(
        shards,
        mesh=fine,
        in_specs=(tokens,) * 6 + (P(), P(), P()),
        out_specs=(tokens,) * 3,
        check_vma=False,
    )
```

```python
import jax
import jax.numpy as jnp
from jax import lax
from jax.experimental import pallas as pl
from jax.experimental.pallas import tpu as pltpu
from jax.sharding import Mesh, PartitionSpec as P

UNIT = 64
TOK = 128
HEADS = 4
DIM = 128
WIDE = HEADS * DIM
NZ = 4
NY = 8
QUNITS = 2 * NZ
KUNITS = NY * TOK // UNIT
GROUP = 8
PAR = 2
MASKS = (0, 2, 1, 3)
ROWS = HEADS * UNIT
AXES = ("y", "zlo", "core", "x", "zhh", "zhl")
bf16 = jnp.bfloat16
f32 = jnp.float32


def pack_kernel(q_ref, d_ref, o_ref, lse_ref, msg_ref):
    msg_ref[:TOK, :WIDE] = q_ref[...]
    msg_ref[:TOK, WIDE:] = d_ref[...]
    lane = lax.broadcasted_iota(jnp.int32, (TOK, DIM), 1)
    delta = jnp.zeros((TOK, DIM), f32)
    for h in range(HEADS):
        cut = slice(h * DIM, (h + 1) * DIM)
        column = jnp.sum(d_ref[:, cut].astype(f32) * o_ref[:, cut].astype(f32), axis=1, keepdims=True)
        delta = jnp.where(lane == h, column, delta)
    delta = delta.T
    line = [lse_ref[h : h + 1, :] for h in range(HEADS)] + [delta[h : h + 1, :] for h in range(HEADS)]
    rest = jnp.concatenate(line, axis=1)
    parts = []
    for _ in range(3):
        low = rest.astype(bf16).astype(f32)
        parts.append(low)
        rest = rest - low
    parts.append(jnp.zeros((5, 2 * WIDE), f32))
    msg_ref[TOK:, :] = jnp.concatenate(parts, axis=0).astype(bf16)


def nt(left, right):
    return lax.dot_general(left, right, (((1,), (1,)), ((), ())), preferred_element_type=f32)


def nn(left, right):
    return lax.dot_general(left, right, (((1,), (0,)), ((), ())), preferred_element_type=f32)


def tile_kernel(cfg, *refs):
    it = iter(refs)

    def take(n):
        return [next(it) for _ in range(n)]

    start, count, s, finals, raws, old_units, has_acc, spread_out = cfg
    rank, need = take(2)
    msgs = take(count)
    kv, kcode, qlim = take(3)
    oldq = next(it) if old_units else None
    old = next(it) if has_acc else None
    gqs = take(len(finals))
    rawq = next(it) if raws else None
    out = next(it)
    qs, ds, lse, delta, ks, kt, kc, gq, work = take(9)
    acc = next(it) if spread_out else out
    base = 2 * start
    units = 2 * count
    chunks = KUNITS // GROUP
    filled = jnp.int32(0)
    for u in range(units):
        for c in range(chunks):
            work[filled] = c * units + u
            active = c * GROUP < need[s * QUNITS + base + u]
            filled = filled + active.astype(jnp.int32)
    rounds = (filled + PAR - 1) // PAR
    for a, m in enumerate(msgs):
        meta = m[TOK : TOK + 8].astype(f32)
        meta = meta[0:1] + meta[1:2] + meta[2:3]
        for half in range(2):
            u = 2 * a + half
            rows = slice(half * UNIT, (half + 1) * UNIT)
            for h in range(HEADS):
                dst = slice(u * ROWS + h * UNIT, u * ROWS + (h + 1) * UNIT)
                qs[dst, :] = m[rows, h * DIM : (h + 1) * DIM]
                ds[dst, :] = m[rows, WIDE + h * DIM : WIDE + (h + 1) * DIM]
            for ref, first in ((lse, 0), (delta, WIDE)):
                cuts = [first + h * TOK + half * UNIT for h in range(HEADS)]
                ref[u] = jnp.concatenate([meta[:, c : c + UNIT] for c in cuts], axis=1)
    gq[...] = jnp.zeros_like(gq)
    if oldq is not None:
        gq[:old_units] = oldq[...]
    acc[...] = jnp.zeros_like(acc) if old is None else old[...]
    spots = []
    for b in range(NY):
        row = kcode[s * NY + b : s * NY + b + 1, :]
        wide = jnp.broadcast_to(row, (TOK, TOK)).T
        for half in range(2):
            i = 2 * b + half
            spot = pl.multiple_of(rank[s * KUNITS + i] * UNIT, UNIT)
            spots.append(spot)
            ks[pl.ds(spot, UNIT), :] = kv[i * UNIT : (i + 1) * UNIT, :]
            kc[pl.ds(spot, UNIT), :] = wide[half * UNIT : (half + 1) * UNIT]
    span = GROUP * UNIT
    for c in range(chunks):
        kt[c] = ks[c * span : (c + 1) * span, :DIM].astype(f32).T.astype(bf16)
    score_scale = DIM ** (-0.5)

    def item(index):
        code = jnp.where(index < filled, work[jnp.minimum(index, filled - 1)], 0)
        u = code % units
        c = code // units
        spot = pl.ds(pl.multiple_of(c * span, span), span)
        keys, vals = ks[spot, :DIM], ks[spot, DIM:]
        at = pl.ds(pl.multiple_of(u * ROWS, ROWS), ROWS)
        q, d = qs[at, :], ds[at, :]
        probs = jnp.exp(nt(keys, q) * score_scale - lse[u])
        kcodes = kc[spot, :]
        mod, pos = kcodes & 3, kcodes >> 2
        lim = jnp.where(index < filled, qlim[base + u], -1)
        bands = []
        for cut in (slice(0, DIM), slice(DIM, ROWS)):
            bound = jnp.where(mod == 0, lim[0:1, cut], jnp.where(mod == 1, lim[1:2, cut], lim[2:3, cut]))
            bands.append(jnp.where(pos <= bound, probs[:, cut], 0.0))
        probs = jnp.concatenate(bands, axis=1)
        grads = probs * (nt(vals, d) - delta[u])
        plow = probs.astype(bf16)
        glow = grads.astype(bf16)
        acc[spot, DIM:] += nn(plow, d)
        acc[spot, :DIM] += nn(glow, q)
        gq[u] += nn(kt[c], glow)

    def body(r, _):
        for j in range(PAR):
            item(r * PAR + j)
        return 0

    lax.fori_loop(0, rounds, body, 0)
    if spread_out:
        for i, spot in enumerate(spots):
            out[i * UNIT : (i + 1) * UNIT, :] = acc[pl.ds(spot, UNIT), :].astype(out.dtype)
    if rawq is not None:
        rawq[...] = gq[raws[0] : raws[1]]
    for (a, _), g in zip(finals, gqs):
        for half in range(2):
            rows = slice(half * UNIT, (half + 1) * UNIT)
            whole = gq[2 * a + half].T
            for h in range(HEADS):
                part = whole[h * UNIT : (h + 1) * UNIT, :]
                g[rows, h * DIM : (h + 1) * DIM] = part.astype(g.dtype)


def in_vmem(value):
    return pltpu.with_memory_space_constraint(value, pltpu.VMEM)


def tile(tables, start, msgs, kv, kcode, qlim, s, finals=(), raws=None, oldq=None, old=None, out_type=None):
    count = len(msgs)
    units = 2 * count
    keys = KUNITS * UNIT
    smem = pl.BlockSpec(memory_space=pltpu.SMEM)
    vmem = pl.BlockSpec(memory_space=pltpu.VMEM)
    arrays = [*msgs, kv, kcode, qlim] + [v for v in (oldq, old) if v is not None]
    outs = [pltpu.VMEM((TOK, WIDE), t) for _, t in finals]
    if raws:
        outs.append(pltpu.VMEM((raws[1] - raws[0], DIM, ROWS), f32))
    outs.append(pltpu.VMEM((keys, 2 * DIM), out_type or f32))
    scratch = [
        pltpu.VMEM((units * ROWS, DIM), bf16),
        pltpu.VMEM((units * ROWS, DIM), bf16),
        pltpu.VMEM((units, 1, ROWS), f32),
        pltpu.VMEM((units, 1, ROWS), f32),
        pltpu.VMEM((keys, 2 * DIM), bf16),
        pltpu.VMEM((KUNITS // GROUP, DIM, GROUP * UNIT), bf16),
        pltpu.VMEM((keys, DIM), jnp.int32),
        pltpu.VMEM((units, DIM, ROWS), f32),
        pltpu.SMEM((units * (KUNITS // GROUP) + 1,), jnp.int32),
    ]
    if out_type:
        scratch.append(pltpu.VMEM((keys, 2 * DIM), f32))
    cfg = (
        start, count, s, finals, raws, 0 if oldq is None else oldq.shape[0], old is not None, out_type is not None
    )

    def body(*refs):
        tile_kernel(cfg, *refs)

    return pl.pallas_call(
        body,
        in_specs=[smem] * 2 + [vmem] * len(arrays),
        out_specs=[vmem] * len(outs),
        out_shape=outs,
        scratch_shapes=scratch,
        compiler_params=pltpu.CompilerParams(vmem_limit_bytes=20 << 20),
    )(*tables, *[in_vmem(v) for v in arrays])


def finish_kernel(parts, key_ref, value_ref):
    total = jnp.sum(parts[...].astype(f32), axis=0)
    key_ref[...] = (total[:, :DIM] * DIM ** (-0.5)).astype(bf16)
    value_ref[...] = total[:, DIM:].astype(bf16)


def copies_kernel(key_ref, value_ref, out):
    for i in range(NY):
        out[i, :, :DIM] = key_ref[...]
        out[i, :, DIM:] = value_ref[...]


def plan(position, modality, table):
    code = (position * 4 + modality).reshape(8, 2, 2, 4, 2, 2, TOK)
    y, zlo, core, x, zhh, zhl = (lax.axis_index(a) for a in AXES)
    kcode = lax.dynamic_slice(code, (0, zlo, 0, x, zhh, zhl, 0), (8, 1, 2, 1, 1, 1, TOK))
    kcode = kcode.reshape(8, 2, TOK)
    kcode = jnp.where(core == 0, jnp.stack([kcode[:, 0], kcode[:, 1]]), jnp.stack([kcode[:, 1], kcode[:, 0]]))
    qcode = lax.dynamic_slice(code, (y, 0, core, x, zhh, 0, 0), (1, 2, 1, 1, 1, 2, TOK)).reshape(4, TOK)
    return tables_of(kcode, qcode, zlo * 2 + zhl, table)


def tables_of(kcode, qcode, own, table):
    masks = jnp.array(MASKS)
    pick = (own ^ masks)[:, None, None] == jnp.arange(4)[None, :, None]
    qcode = jnp.sum(jnp.where(pick, qcode[None], 0), axis=1)
    qpos, qmod = (qcode >> 2).reshape(QUNITS, UNIT), (qcode & 3).reshape(QUNITS, UNIT)
    bids = [
        jnp.where(qmod == 0, table[0, m], jnp.where(qmod == 1, table[1, m], table[2, m])) for m in range(3)
    ]
    lim = jnp.stack([jnp.where(b == 1, qpos | (UNIT - 1), qpos) for b in bids], axis=1)
    qlim = jnp.concatenate([lim] * HEADS, axis=2)
    kunit = (kcode >> 2).reshape(2, KUNITS, UNIT)
    low = jnp.min(kunit, axis=2)
    index = jnp.arange(KUNITS)
    a, b = low[:, None, :], low[:, :, None]
    before = (a < b) | ((a == b) & (index[None, None, :] < index[None, :, None]))
    rank = jnp.sum(before.astype(jnp.int32), axis=2)
    qhigh = jnp.max(qpos, axis=1)
    need = jnp.sum((a // UNIT <= qhigh[None, :, None] // UNIT).astype(jnp.int32), axis=2)
    return (rank.reshape(-1), need.reshape(-1)), kcode.reshape(2 * NY, TOK), qlim


def shards(queries, grad_out, attn_out, key_states, value_states, log_norm, position, modality, table):
    def along_z(value, mask):
        return lax.ppermute(value, ("zlo", "zhl"), [(i, i ^ mask) for i in range(NZ)])

    def other_core(value):
        return lax.ppermute(value, "core", [(0, 1), (1, 0)])

    def over_y(value):
        return lax.all_to_all(value, "y", 0, 0)

    copies = pl.pallas_call(
        copies_kernel,
        out_shape=jax.ShapeDtypeStruct((NY, TOK, 2 * DIM), bf16),
        compiler_params=pltpu.CompilerParams(vmem_limit_bytes=8 << 20),
        name="copies",
    )(key_states, value_states)
    copies, queries = lax.optimization_barrier((copies, queries))
    msg = pl.pallas_call(
        pack_kernel, out_shape=pltpu.VMEM((TOK + 8, 2 * WIDE), bf16), compiler_params=pltpu.CompilerParams(vmem_limit_bytes=8 << 20), name="pack"
    )(queries, grad_out, attn_out, log_norm.T)
    kvo = over_y(copies).reshape(NY * TOK, 2 * DIM)
    near = along_z(msg, MASKS[1])
    far, last = along_z(msg, MASKS[2]), along_z(msg, MASKS[3])
    tables, kcode, qlim = plan(position, modality, table)
    kvo, tables, kcode, qlim = lax.optimization_barrier((kvo, tables, kcode, qlim))
    kvx = other_core(kvo)
    raw_near, old = tile(tables, 0, (msg, near), kvo, kcode, qlim, 0, raws=(0, 4))
    own_q, near_q, raw_far, gkvx = tile(
        tables, 0, (msg, near, far, last), kvx, kcode, qlim, 1,
        ((0, f32), (1, bf16)), (4, 8), raw_near, None, bf16,
    )
    got = other_core(gkvx)
    far_q, last_q, gkvo = tile(
        tables, 2, (far, last), kvo, kcode, qlim, 0, ((0, bf16), (1, bf16)), None, raw_far, old, f32
    )
    paired = (gkvo + got.astype(f32)).astype(bf16).reshape(NY, TOK, 2 * DIM)
    summed = over_y(paired)
    narrow = jax.ShapeDtypeStruct((TOK, DIM), bf16)
    grad_key, grad_value = pl.pallas_call(
        finish_kernel, out_shape=[narrow] * 2, compiler_params=pltpu.CompilerParams(vmem_limit_bytes=8 << 20), name="finish"
    )(in_vmem(summed))
    back = [along_z(near_q, MASKS[1])]
    back += [along_z(far_q, MASKS[2]), along_z(last_q, MASKS[3])]
    g0 = own_q
    score_scale = DIM ** (-0.5)
    grad_q = (g0 + back[0].astype(f32) + back[1].astype(f32) + back[2].astype(f32)) * score_scale
    return grad_q.astype(bf16), grad_key, grad_value


def solution(mesh):
    fine = Mesh(mesh.devices.reshape(8, 2, 2, 4, 2, 2), AXES)
    tokens = P(AXES, None)

    return jax.shard_map(
        shards,
        mesh=fine,
        in_specs=(tokens,) * 6 + (P(), P(), P()),
        out_specs=(tokens,) * 3,
        check_vma=False,
    )
```

```python
import jax
import jax.numpy as jnp
from jax import lax
from jax.experimental import pallas as pl
from jax.experimental.pallas import tpu as pltpu
from jax.sharding import Mesh, PartitionSpec as P

UNIT = 64
TOK = 128
HEADS = 4
DIM = 128
WIDE = HEADS * DIM
NZ = 4
NY = 8
QUNITS = 2 * NZ
KUNITS = NY * TOK // UNIT
GROUP = 8
PAR = 2
MASKS = (0, 2, 1, 3)
ROWS = HEADS * UNIT
AXES = ("y", "zlo", "core", "x", "zhh", "zhl")
bf16 = jnp.bfloat16
f32 = jnp.float32


def pack_kernel(q_ref, d_ref, o_ref, lse_ref, msg_ref):
    msg_ref[:TOK, :WIDE] = q_ref[...]
    msg_ref[:TOK, WIDE:] = d_ref[...]
    lane = lax.broadcasted_iota(jnp.int32, (TOK, DIM), 1)
    delta = jnp.zeros((TOK, DIM), f32)
    for h in range(HEADS):
        cut = slice(h * DIM, (h + 1) * DIM)
        column = jnp.sum(d_ref[:, cut].astype(f32) * o_ref[:, cut].astype(f32), axis=1, keepdims=True)
        delta = jnp.where(lane == h, column, delta)
    delta = delta.T
    line = [lse_ref[h : h + 1, :] for h in range(HEADS)] + [delta[h : h + 1, :] for h in range(HEADS)]
    rest = jnp.concatenate(line, axis=1)
    parts = []
    for _ in range(3):
        low = rest.astype(bf16).astype(f32)
        parts.append(low)
        rest = rest - low
    parts.append(jnp.zeros((5, 2 * WIDE), f32))
    msg_ref[TOK:, :] = jnp.concatenate(parts, axis=0).astype(bf16)


def nt(left, right):
    return lax.dot_general(left, right, (((1,), (1,)), ((), ())), preferred_element_type=f32)


def nn(left, right):
    return lax.dot_general(left, right, (((1,), (0,)), ((), ())), preferred_element_type=f32)


def tile_kernel(cfg, *refs):
    it = iter(refs)

    def take(n):
        return [next(it) for _ in range(n)]

    start, count, s, finals, raws, old_units, has_acc, spread_out = cfg
    rank, need = take(2)
    msgs = take(count)
    kv, kcode, qlim = take(3)
    oldq = next(it) if old_units else None
    old = next(it) if has_acc else None
    gqs = take(len(finals))
    rawq = next(it) if raws else None
    out = next(it)
    qs, ds, lse, delta, ks, kt, kc, gq, work = take(9)
    acc = next(it) if spread_out else out
    base = 2 * start
    units = 2 * count
    chunks = KUNITS // GROUP
    filled = jnp.int32(0)
    for u in range(units):
        for c in range(chunks):
            work[filled] = c * units + u
            active = c * GROUP < need[s * QUNITS + base + u]
            filled = filled + active.astype(jnp.int32)
    rounds = (filled + PAR - 1) // PAR
    for a, m in enumerate(msgs):
        meta = m[TOK : TOK + 8].astype(f32)
        meta = meta[0:1] + meta[1:2] + meta[2:3]
        for half in range(2):
            u = 2 * a + half
            rows = slice(half * UNIT, (half + 1) * UNIT)
            for h in range(HEADS):
                dst = slice(u * ROWS + h * UNIT, u * ROWS + (h + 1) * UNIT)
                qs[dst, :] = m[rows, h * DIM : (h + 1) * DIM]
                ds[dst, :] = m[rows, WIDE + h * DIM : WIDE + (h + 1) * DIM]
            for ref, first in ((lse, 0), (delta, WIDE)):
                cuts = [first + h * TOK + half * UNIT for h in range(HEADS)]
                ref[u] = jnp.concatenate([meta[:, c : c + UNIT] for c in cuts], axis=1)
    gq[...] = jnp.zeros_like(gq)
    if oldq is not None:
        gq[:old_units] = oldq[...]
    acc[...] = jnp.zeros_like(acc) if old is None else old[...]
    spots = []
    for b in range(NY):
        row = kcode[s * NY + b : s * NY + b + 1, :]
        wide = jnp.broadcast_to(row, (TOK, TOK)).T
        for half in range(2):
            i = 2 * b + half
            spot = pl.multiple_of(rank[s * KUNITS + i] * UNIT, UNIT)
            spots.append(spot)
            ks[pl.ds(spot, UNIT), :] = kv[i * UNIT : (i + 1) * UNIT, :]
            kc[pl.ds(spot, UNIT), :] = wide[half * UNIT : (half + 1) * UNIT]
    span = GROUP * UNIT
    for c in range(chunks):
        kt[c] = ks[c * span : (c + 1) * span, :DIM].astype(f32).T.astype(bf16)
    score_scale = DIM ** (-0.5)

    def item(index):
        code = jnp.where(index < filled, work[jnp.minimum(index, filled - 1)], 0)
        u = code % units
        c = code // units
        spot = pl.ds(pl.multiple_of(c * span, span), span)
        keys, vals = ks[spot, :DIM], ks[spot, DIM:]
        at = pl.ds(pl.multiple_of(u * ROWS, ROWS), ROWS)
        q, d = qs[at, :], ds[at, :]
        probs = jnp.exp(nt(keys, q) * score_scale - lse[u])
        kcodes = kc[spot, :]
        mod, pos = kcodes & 3, kcodes >> 2
        lim = jnp.where(index < filled, qlim[base + u], -1)
        bands = []
        for cut in (slice(0, DIM), slice(DIM, ROWS)):
            bound = jnp.where(mod == 0, lim[0:1, cut], jnp.where(mod == 1, lim[1:2, cut], lim[2:3, cut]))
            bands.append(jnp.where(pos <= bound, probs[:, cut], 0.0))
        probs = jnp.concatenate(bands, axis=1)
        grads = probs * (nt(vals, d) - delta[u])
        plow = probs.astype(bf16)
        glow = grads.astype(bf16)
        acc[spot, DIM:] += nn(plow, d)
        acc[spot, :DIM] += nn(glow, q)
        gq[u] += nn(kt[c], glow)

    def body(r, _):
        for j in range(PAR):
            item(r * PAR + j)
        return 0

    lax.fori_loop(0, rounds, body, 0)
    if spread_out:
        for i, spot in enumerate(spots):
            out[i * UNIT : (i + 1) * UNIT, :] = acc[pl.ds(spot, UNIT), :].astype(out.dtype)
    if rawq is not None:
        rawq[...] = gq[raws[0] : raws[1]]
    for (a, _), g in zip(finals, gqs):
        for half in range(2):
            rows = slice(half * UNIT, (half + 1) * UNIT)
            whole = gq[2 * a + half].T
            for h in range(HEADS):
                part = whole[h * UNIT : (h + 1) * UNIT, :]
                g[rows, h * DIM : (h + 1) * DIM] = part.astype(g.dtype)


def in_vmem(value):
    return pltpu.with_memory_space_constraint(value, pltpu.VMEM)


def tile(tables, start, msgs, kv, kcode, qlim, s, finals=(), raws=None, oldq=None, old=None, out_type=None):
    count = len(msgs)
    units = 2 * count
    keys = KUNITS * UNIT
    smem = pl.BlockSpec(memory_space=pltpu.SMEM)
    vmem = pl.BlockSpec(memory_space=pltpu.VMEM)
    arrays = [*msgs, kv, kcode, qlim] + [v for v in (oldq, old) if v is not None]
    outs = [pltpu.VMEM((TOK, WIDE), t) for _, t in finals]
    if raws:
        outs.append(pltpu.VMEM((raws[1] - raws[0], DIM, ROWS), f32))
    outs.append(pltpu.VMEM((keys, 2 * DIM), out_type or f32))
    scratch = [
        pltpu.VMEM((units * ROWS, DIM), bf16),
        pltpu.VMEM((units * ROWS, DIM), bf16),
        pltpu.VMEM((units, 1, ROWS), f32),
        pltpu.VMEM((units, 1, ROWS), f32),
        pltpu.VMEM((keys, 2 * DIM), bf16),
        pltpu.VMEM((KUNITS // GROUP, DIM, GROUP * UNIT), bf16),
        pltpu.VMEM((keys, DIM), jnp.int32),
        pltpu.VMEM((units, DIM, ROWS), f32),
        pltpu.SMEM((units * (KUNITS // GROUP) + 1,), jnp.int32),
    ]
    if out_type:
        scratch.append(pltpu.VMEM((keys, 2 * DIM), f32))
    cfg = (
        start, count, s, finals, raws, 0 if oldq is None else oldq.shape[0], old is not None, out_type is not None
    )

    def body(*refs):
        tile_kernel(cfg, *refs)

    return pl.pallas_call(
        body,
        in_specs=[smem] * 2 + [vmem] * len(arrays),
        out_specs=[vmem] * len(outs),
        out_shape=outs,
        scratch_shapes=scratch,
        compiler_params=pltpu.CompilerParams(vmem_limit_bytes=20 << 20),
    )(*tables, *[in_vmem(v) for v in arrays])


def finish_kernel(parts, key_ref, value_ref):
    total = jnp.sum(parts[...].astype(f32), axis=0)
    key_ref[...] = (total[:, :DIM] * DIM ** (-0.5)).astype(bf16)
    value_ref[...] = total[:, DIM:].astype(bf16)


def copies_kernel(key_ref, value_ref, out, sems):
    moves = []
    for i in range(NY):
        for j, ref in enumerate((key_ref, value_ref)):
            half = out.at[i, :, j * DIM : (j + 1) * DIM]
            moves.append(pltpu.make_async_copy(ref, half, sems.at[2 * i + j]))
    for move in moves:
        move.start()
    for move in moves:
        move.wait()


def plan(position, modality, table):
    code = (position * 4 + modality).reshape(8, 2, 2, 4, 2, 2, TOK)
    y, zlo, core, x, zhh, zhl = (lax.axis_index(a) for a in AXES)
    kcode = lax.dynamic_slice(code, (0, zlo, 0, x, zhh, zhl, 0), (8, 1, 2, 1, 1, 1, TOK))
    kcode = kcode.reshape(8, 2, TOK)
    kcode = jnp.where(core == 0, jnp.stack([kcode[:, 0], kcode[:, 1]]), jnp.stack([kcode[:, 1], kcode[:, 0]]))
    qcode = lax.dynamic_slice(code, (y, 0, core, x, zhh, 0, 0), (1, 2, 1, 1, 1, 2, TOK)).reshape(4, TOK)
    return tables_of(kcode, qcode, zlo * 2 + zhl, table)


def tables_of(kcode, qcode, own, table):
    masks = jnp.array(MASKS)
    pick = (own ^ masks)[:, None, None] == jnp.arange(4)[None, :, None]
    qcode = jnp.sum(jnp.where(pick, qcode[None], 0), axis=1)
    qpos, qmod = (qcode >> 2).reshape(QUNITS, UNIT), (qcode & 3).reshape(QUNITS, UNIT)
    bids = [
        jnp.where(qmod == 0, table[0, m], jnp.where(qmod == 1, table[1, m], table[2, m])) for m in range(3)
    ]
    lim = jnp.stack([jnp.where(b == 1, qpos | (UNIT - 1), qpos) for b in bids], axis=1)
    qlim = jnp.concatenate([lim] * HEADS, axis=2)
    kunit = (kcode >> 2).reshape(2, KUNITS, UNIT)
    low = jnp.min(kunit, axis=2)
    index = jnp.arange(KUNITS)
    a, b = low[:, None, :], low[:, :, None]
    before = (a < b) | ((a == b) & (index[None, None, :] < index[None, :, None]))
    rank = jnp.sum(before.astype(jnp.int32), axis=2)
    qhigh = jnp.max(qpos, axis=1)
    need = jnp.sum((a // UNIT <= qhigh[None, :, None] // UNIT).astype(jnp.int32), axis=2)
    return (rank.reshape(-1), need.reshape(-1)), kcode.reshape(2 * NY, TOK), qlim


def shards(queries, grad_out, attn_out, key_states, value_states, log_norm, position, modality, table):
    def along_z(value, mask):
        return lax.ppermute(value, ("zlo", "zhl"), [(i, i ^ mask) for i in range(NZ)])

    def other_core(value):
        return lax.ppermute(value, "core", [(0, 1), (1, 0)])

    def over_y(value):
        return lax.all_to_all(value, "y", 0, 0)

    copies = pl.pallas_call(
        copies_kernel,
        out_shape=jax.ShapeDtypeStruct((NY, TOK, 2 * DIM), bf16),
        in_specs=[pl.BlockSpec(memory_space=pltpu.HBM)] * 2,
        out_specs=pl.BlockSpec(memory_space=pltpu.HBM),
        scratch_shapes=[pltpu.SemaphoreType.DMA((2 * NY,))],
        compiler_params=pltpu.CompilerParams(vmem_limit_bytes=8 << 20),
        name="copies",
    )(key_states, value_states)
    copies, queries = lax.optimization_barrier((copies, queries))
    msg = pl.pallas_call(
        pack_kernel, out_shape=pltpu.VMEM((TOK + 8, 2 * WIDE), bf16), compiler_params=pltpu.CompilerParams(vmem_limit_bytes=8 << 20), name="pack"
    )(queries, grad_out, attn_out, log_norm.T)
    kvo = over_y(copies).reshape(NY * TOK, 2 * DIM)
    near = along_z(msg, MASKS[1])
    far, last = along_z(msg, MASKS[2]), along_z(msg, MASKS[3])
    tables, kcode, qlim = plan(position, modality, table)
    kvo, tables, kcode, qlim = lax.optimization_barrier((kvo, tables, kcode, qlim))
    kvx = other_core(kvo)
    raw_near, old = tile(tables, 0, (msg, near), kvo, kcode, qlim, 0, raws=(0, 4))
    own_q, near_q, raw_far, gkvx = tile(
        tables, 0, (msg, near, far, last), kvx, kcode, qlim, 1,
        ((0, f32), (1, bf16)), (4, 8), raw_near, None, bf16,
    )
    got = other_core(gkvx)
    far_q, last_q, gkvo = tile(
        tables, 2, (far, last), kvo, kcode, qlim, 0, ((0, bf16), (1, bf16)), None, raw_far, old, f32
    )
    paired = (gkvo + got.astype(f32)).astype(bf16).reshape(NY, TOK, 2 * DIM)
    summed = over_y(paired)
    narrow = jax.ShapeDtypeStruct((TOK, DIM), bf16)
    grad_key, grad_value = pl.pallas_call(
        finish_kernel, out_shape=[narrow] * 2, compiler_params=pltpu.CompilerParams(vmem_limit_bytes=8 << 20), name="finish"
    )(in_vmem(summed))
    back = [along_z(near_q, MASKS[1])]
    back += [along_z(far_q, MASKS[2]), along_z(last_q, MASKS[3])]
    g0 = own_q
    score_scale = DIM ** (-0.5)
    grad_q = (g0 + back[0].astype(f32) + back[1].astype(f32) + back[2].astype(f32)) * score_scale
    return grad_q.astype(bf16), grad_key, grad_value


def solution(mesh):
    fine = Mesh(mesh.devices.reshape(8, 2, 2, 4, 2, 2), AXES)
    tokens = P(AXES, None)

    return jax.shard_map(
        shards,
        mesh=fine,
        in_specs=(tokens,) * 6 + (P(), P(), P()),
        out_specs=(tokens,) * 3,
        check_vma=False,
    )
```

```python
import jax
import jax.numpy as jnp
from jax import lax
from jax.experimental import pallas as pl
from jax.experimental.pallas import tpu as pltpu
from jax.sharding import Mesh, PartitionSpec as P

UNIT = 64
TOK = 128
HEADS = 4
DIM = 128
WIDE = HEADS * DIM
NZ = 4
NY = 8
QUNITS = 2 * NZ
KUNITS = NY * TOK // UNIT
GROUP = 8
PAR = 2
MASKS = (0, 2, 1, 3)
ROWS = HEADS * UNIT
AXES = ("y", "zlo", "core", "x", "zhh", "zhl")
bf16 = jnp.bfloat16
f32 = jnp.float32


def pack_kernel(q_ref, d_ref, o_ref, lse_ref, msg_ref):
    msg_ref[:TOK, :WIDE] = q_ref[...]
    msg_ref[:TOK, WIDE:] = d_ref[...]
    lane = lax.broadcasted_iota(jnp.int32, (TOK, DIM), 1)
    delta = jnp.zeros((TOK, DIM), f32)
    for h in range(HEADS):
        cut = slice(h * DIM, (h + 1) * DIM)
        column = jnp.sum(d_ref[:, cut].astype(f32) * o_ref[:, cut].astype(f32), axis=1, keepdims=True)
        delta = jnp.where(lane == h, column, delta)
    delta = delta.T
    line = [lse_ref[h : h + 1, :] for h in range(HEADS)] + [delta[h : h + 1, :] for h in range(HEADS)]
    rest = jnp.concatenate(line, axis=1)
    parts = []
    for _ in range(3):
        low = rest.astype(bf16).astype(f32)
        parts.append(low)
        rest = rest - low
    parts.append(jnp.zeros((5, 2 * WIDE), f32))
    msg_ref[TOK:, :] = jnp.concatenate(parts, axis=0).astype(bf16)


def nt(left, right):
    return lax.dot_general(left, right, (((1,), (1,)), ((), ())), preferred_element_type=f32)


def nn(left, right):
    return lax.dot_general(left, right, (((1,), (0,)), ((), ())), preferred_element_type=f32)


def tile_kernel(cfg, *refs):
    it = iter(refs)

    def take(n):
        return [next(it) for _ in range(n)]

    start, count, s, finals, raws, old_units, has_acc, spread_out = cfg
    tab = next(it)
    msgs = take(count)
    kv, kcode, qlim = take(3)
    oldq = next(it) if old_units else None
    old = next(it) if has_acc else None
    gqs = take(len(finals))
    rawq = next(it) if raws else None
    out = next(it)
    qs, ds, lse, delta, ks, kt, kc, gq, work = take(9)
    acc = next(it) if spread_out else out
    base = 2 * start
    units = 2 * count
    chunks = KUNITS // GROUP
    filled = jnp.int32(0)
    for u in range(units):
        for c in range(chunks):
            work[filled] = c * units + u
            active = c * GROUP < tab[2 * KUNITS + s * QUNITS + base + u, 0]
            filled = filled + active.astype(jnp.int32)
    rounds = (filled + PAR - 1) // PAR
    for a, m in enumerate(msgs):
        meta = m[TOK : TOK + 8, :].astype(f32)
        meta = meta[0:1] + meta[1:2] + meta[2:3]
        for half in range(2):
            u = 2 * a + half
            rows = slice(half * UNIT, (half + 1) * UNIT)
            for h in range(HEADS):
                dst = slice(u * ROWS + h * UNIT, u * ROWS + (h + 1) * UNIT)
                qs[dst, :] = m[rows, h * DIM : (h + 1) * DIM]
                ds[dst, :] = m[rows, WIDE + h * DIM : WIDE + (h + 1) * DIM]
            for ref, first in ((lse, 0), (delta, WIDE)):
                cuts = [first + h * TOK + half * UNIT for h in range(HEADS)]
                ref[u] = jnp.concatenate([meta[:, c : c + UNIT] for c in cuts], axis=1)
    gq[...] = jnp.zeros_like(gq)
    if oldq is not None:
        gq[:old_units] = oldq[...]
    acc[...] = jnp.zeros_like(acc) if old is None else old[...]
    spots = []
    for b in range(NY):
        row = kcode[s * NY + b : s * NY + b + 1, :]
        wide = jnp.broadcast_to(row, (TOK, TOK)).T
        for half in range(2):
            i = half * NY + b
            spot = pl.multiple_of(tab[s * KUNITS + i, 0] * UNIT, UNIT)
            nat = slice(b * TOK + half * UNIT, b * TOK + (half + 1) * UNIT)
            spots.append((nat, spot))
            ks[pl.ds(spot, UNIT), :] = kv[nat, :]
            kc[pl.ds(spot, UNIT), :] = wide[half * UNIT : (half + 1) * UNIT]
    span = GROUP * UNIT
    for c in range(chunks):
        kt[c] = ks[c * span : (c + 1) * span, :DIM].astype(f32).T.astype(bf16)
    score_scale = DIM ** (-0.5)

    def item(index):
        code = jnp.where(index < filled, work[jnp.minimum(index, filled - 1)], 0)
        u = code % units
        c = code // units
        spot = pl.ds(pl.multiple_of(c * span, span), span)
        keys, vals = ks[spot, :DIM], ks[spot, DIM:]
        at = pl.ds(pl.multiple_of(u * ROWS, ROWS), ROWS)
        q, d = qs[at, :], ds[at, :]
        probs = jnp.exp(nt(keys, q) * score_scale - lse[u])
        kcodes = kc[spot, :]
        mod, pos = kcodes & 3, kcodes >> 2
        lim = jnp.where(index < filled, qlim[base + u], -1)
        bands = []
        for cut in (slice(0, DIM), slice(DIM, ROWS)):
            bound = jnp.where(mod == 0, lim[0:1, cut], jnp.where(mod == 1, lim[1:2, cut], lim[2:3, cut]))
            bands.append(jnp.where(pos <= bound, probs[:, cut], 0.0))
        probs = jnp.concatenate(bands, axis=1)
        grads = probs * (nt(vals, d) - delta[u])
        plow = probs.astype(bf16)
        glow = grads.astype(bf16)
        acc[spot, DIM:] += nn(plow, d)
        acc[spot, :DIM] += nn(glow, q)
        gq[u] += nn(kt[c], glow)

    def body(r, _):
        for j in range(PAR):
            item(r * PAR + j)
        return 0

    lax.fori_loop(0, rounds, body, 0)
    if spread_out:
        for nat, spot in spots:
            out[nat, :] = acc[pl.ds(spot, UNIT), :].astype(out.dtype)
    if rawq is not None:
        rawq[...] = gq[raws[0] : raws[1]]
    for (a, _), g in zip(finals, gqs):
        for half in range(2):
            rows = slice(half * UNIT, (half + 1) * UNIT)
            whole = gq[2 * a + half].T
            for h in range(HEADS):
                part = whole[h * UNIT : (h + 1) * UNIT, :]
                g[rows, h * DIM : (h + 1) * DIM] = part.astype(g.dtype)


def in_vmem(value):
    return pltpu.with_memory_space_constraint(value, pltpu.VMEM)


def tile(tab, start, msgs, kv, kcode, qlim, s, finals=(), raws=None, oldq=None, old=None, out_type=None):
    count = len(msgs)
    units = 2 * count
    keys = KUNITS * UNIT
    smem = pl.BlockSpec(memory_space=pltpu.SMEM)
    vmem = pl.BlockSpec(memory_space=pltpu.VMEM)
    arrays = [*msgs, kv, kcode, qlim] + [v for v in (oldq, old) if v is not None]
    outs = [pltpu.VMEM((TOK, WIDE), t) for _, t in finals]
    if raws:
        outs.append(pltpu.VMEM((raws[1] - raws[0], DIM, ROWS), f32))
    outs.append(pltpu.VMEM((keys, 2 * DIM), out_type or f32))
    scratch = [
        pltpu.VMEM((units * ROWS, DIM), bf16),
        pltpu.VMEM((units * ROWS, DIM), bf16),
        pltpu.VMEM((units, 1, ROWS), f32),
        pltpu.VMEM((units, 1, ROWS), f32),
        pltpu.VMEM((keys, 2 * DIM), bf16),
        pltpu.VMEM((KUNITS // GROUP, DIM, GROUP * UNIT), bf16),
        pltpu.VMEM((keys, DIM), jnp.int32),
        pltpu.VMEM((units, DIM, ROWS), f32),
        pltpu.SMEM((units * (KUNITS // GROUP) + 1,), jnp.int32),
    ]
    if out_type:
        scratch.append(pltpu.VMEM((keys, 2 * DIM), f32))
    cfg = (
        start, count, s, finals, raws, 0 if oldq is None else oldq.shape[0], old is not None, out_type is not None
    )

    def body(*refs):
        tile_kernel(cfg, *refs)

    return pl.pallas_call(
        body,
        in_specs=[smem] + [vmem] * len(arrays),
        out_specs=[vmem] * len(outs),
        out_shape=outs,
        scratch_shapes=scratch,
        compiler_params=pltpu.CompilerParams(vmem_limit_bytes=20 << 20),
    )(tab, *[in_vmem(v) for v in arrays])


def finish_kernel(parts, key_ref, value_ref):
    total = jnp.sum(parts[...].astype(f32), axis=0)
    key_ref[...] = (total[:, :DIM] * DIM ** (-0.5)).astype(bf16)
    value_ref[...] = total[:, DIM:].astype(bf16)


def unit_low(value, fold, fill):
    lane = lax.broadcasted_iota(jnp.int32, value.shape, 1)
    first = fold(jnp.where(lane < UNIT, value, fill), axis=1, keepdims=True)
    second = fold(jnp.where(lane < UNIT, fill, value), axis=1, keepdims=True)
    return first, second


def plan_kernel(table, position, modality, tab, kcode, qlim, rows, sems):
    y, zlo, core, x, zhh, zhl = (lax.axis_index(a) for a in AXES)

    def line(y, zlo, core, zhl):
        return ((((y * 2 + zlo) * 2 + core) * 4 + x) * 2 + zhh) * 2 + zhl

    lines = [line(b, zlo, core ^ s, zhl) for s in range(2) for b in range(NY)]
    lines += [line(y, zlo ^ (mask >> 1), core, zhl ^ (mask & 1)) for mask in MASKS]
    moves = []
    for i, at in enumerate(lines):
        for j, ref in enumerate((position, modality)):
            moves.append(pltpu.make_async_copy(ref.at[at], rows.at[j, i], sems.at[j, i]))
    for move in moves:
        move.start()
    for move in moves:
        move.wait()
    pos = jnp.concatenate([rows[0, i] for i in range(len(lines))], axis=0)
    mod = jnp.concatenate([rows[1, i] for i in range(len(lines))], axis=0)
    keys = 2 * NY
    kcode[...] = pos[:keys] * 4 + mod[:keys]
    low = unit_low(pos[:keys], jnp.min, 1 << 20)
    high = unit_low(pos[keys:], jnp.max, -1)
    qlast = jnp.concatenate(
        [high[half][a : a + 1] for a in range(NZ) for half in range(2)], axis=0
    )
    qlast = jnp.broadcast_to(qlast, (QUNITS, TOK)) >> 6
    lane = lax.broadcasted_iota(jnp.int32, (KUNITS, TOK), 1)
    index = lax.broadcasted_iota(jnp.int32, (KUNITS, TOK), 0)
    for s in range(2):
        part = slice(s * NY, (s + 1) * NY)
        column = jnp.broadcast_to(jnp.concatenate([low[0][part], low[1][part]], axis=0), (KUNITS, TOK))
        square = jnp.concatenate([column, jnp.zeros((TOK - KUNITS, TOK), jnp.int32)], axis=0).T
        across = square[:KUNITS]
        before = ((across < column) | ((across == column) & (lane < index))) & (lane < KUNITS)
        rank = jnp.sum(before.astype(jnp.int32), axis=1, keepdims=True)
        tab[s * KUNITS : (s + 1) * KUNITS, :] = jnp.broadcast_to(rank, (KUNITS, TOK))
        seen = ((across[:QUNITS] >> 6) <= qlast) & (lane[:QUNITS] < KUNITS)
        need = jnp.sum(seen.astype(jnp.int32), axis=1, keepdims=True)
        at = 2 * KUNITS + s * QUNITS
        tab[at : at + QUNITS, :] = jnp.broadcast_to(need, (QUNITS, TOK))
    qpos, qmod = pos[keys:], mod[keys:]
    for m in range(3):
        bid = jnp.where(qmod == 0, table[0, m], jnp.where(qmod == 1, table[1, m], table[2, m]))
        lim = jnp.where(bid == 1, qpos | (UNIT - 1), qpos)
        for a in range(NZ):
            for half in range(2):
                cut = lim[a : a + 1, half * UNIT : (half + 1) * UNIT]
                qlim[2 * a + half, m : m + 1, :] = jnp.concatenate([cut] * HEADS, axis=1)


def plan(position, modality, table):
    hbm = pl.BlockSpec(memory_space=pltpu.HBM)
    vmem = pl.BlockSpec(memory_space=pltpu.VMEM)
    count = 2 * NY + NZ
    lines = position.shape[0] // TOK
    return pl.pallas_call(
        plan_kernel,
        in_specs=[pl.BlockSpec(memory_space=pltpu.SMEM), hbm, hbm],
        out_specs=[vmem] * 3,
        out_shape=[
            jax.ShapeDtypeStruct((2 * KUNITS + 2 * QUNITS, TOK), jnp.int32),
            pltpu.VMEM((2 * NY, TOK), jnp.int32),
            pltpu.VMEM((QUNITS, 3, ROWS), jnp.int32),
        ],
        scratch_shapes=[
            pltpu.VMEM((2, count, 1, TOK), jnp.int32),
            pltpu.SemaphoreType.DMA((2, count)),
        ],
        compiler_params=pltpu.CompilerParams(vmem_limit_bytes=8 << 20),
        name="plan",
    )(table, position.reshape(lines, 1, TOK), modality.reshape(lines, 1, TOK))


def shards(queries, grad_out, attn_out, key_states, value_states, log_norm, position, modality, table):
    def along_z(value, mask):
        return lax.ppermute(value, ("zlo", "zhl"), [(i, i ^ mask) for i in range(NZ)])

    def other_core(value):
        return lax.ppermute(value, "core", [(0, 1), (1, 0)])

    def over_y(value):
        return lax.all_to_all(value, "y", 0, 0)

    pair = jnp.concatenate([key_states, value_states], axis=1)
    copies = jnp.broadcast_to(pair[None], (NY, TOK, 2 * DIM))
    msg = pl.pallas_call(
        pack_kernel, out_shape=pltpu.VMEM((TOK + 8, 2 * WIDE), bf16), compiler_params=pltpu.CompilerParams(vmem_limit_bytes=8 << 20), name="pack"
    )(queries, grad_out, attn_out, log_norm.T)
    far, last = along_z(msg, MASKS[2]), along_z(msg, MASKS[3])
    kvo = over_y(copies).reshape(NY * TOK, 2 * DIM)
    near = along_z(msg, MASKS[1])
    tab, kcode, qlim = plan(position, modality, table)
    kvx = other_core(kvo)
    raw_near, old = tile(tab, 0, (msg, near), kvo, kcode, qlim, 0, raws=(0, 4))
    own_q, near_q, raw_far, gkvx = tile(
        tab, 0, (msg, near, far, last), kvx, kcode, qlim, 1,
        ((0, f32), (1, bf16)), (4, 8), raw_near, None, bf16,
    )
    got = other_core(gkvx)
    far_q, last_q, gkvo = tile(
        tab, 2, (far, last), kvo, kcode, qlim, 0, ((0, bf16), (1, bf16)), None, raw_far, old, f32
    )
    paired = (gkvo + got.astype(f32)).astype(bf16).reshape(NY, TOK, 2 * DIM)
    summed = over_y(paired)
    narrow = jax.ShapeDtypeStruct((TOK, DIM), bf16)
    grad_key, grad_value = pl.pallas_call(
        finish_kernel, out_shape=[narrow] * 2, compiler_params=pltpu.CompilerParams(vmem_limit_bytes=8 << 20), name="finish"
    )(in_vmem(summed))
    back = [along_z(g, mask) for g, mask in zip((near_q, far_q, last_q), MASKS[1:])]
    grad_q = (own_q + back[0].astype(f32) + back[1].astype(f32) + back[2].astype(f32)) * DIM ** (-0.5)
    return grad_q.astype(bf16), grad_key, grad_value


def solution(mesh):
    fine = Mesh(mesh.devices.reshape(8, 2, 2, 4, 2, 2), AXES)
    tokens = P(AXES, None)

    return jax.shard_map(
        shards,
        mesh=fine,
        in_specs=(tokens,) * 6 + (P(), P(), P()),
        out_specs=(tokens,) * 3,
        check_vma=False,
    )
```

```python
import jax
import jax.numpy as jnp
from jax import lax
from jax.experimental import pallas as pl
from jax.experimental.pallas import tpu as pltpu
from jax.sharding import Mesh, PartitionSpec as P

UNIT = 64
TOK = 128
HEADS = 4
DIM = 128
WIDE = HEADS * DIM
NZ = 4
NY = 8
QUNITS = 2 * NZ
KUNITS = NY * TOK // UNIT
GROUP = 8
PAR = 2
MASKS = (0, 2, 1, 3)
ROWS = HEADS * UNIT
AXES = ("y", "zlo", "core", "x", "zhh", "zhl")
bf16 = jnp.bfloat16
f32 = jnp.float32


def pack_kernel(q_ref, d_ref, o_ref, lse_ref, msg_ref):
    msg_ref[:TOK, :WIDE] = q_ref[...]
    msg_ref[:TOK, WIDE:] = d_ref[...]
    lane = lax.broadcasted_iota(jnp.int32, (TOK, DIM), 1)
    delta = jnp.zeros((TOK, DIM), f32)
    for h in range(HEADS):
        cut = slice(h * DIM, (h + 1) * DIM)
        column = jnp.sum(d_ref[:, cut].astype(f32) * o_ref[:, cut].astype(f32), axis=1, keepdims=True)
        delta = jnp.where(lane == h, column, delta)
    delta = delta.T
    line = [lse_ref[h : h + 1, :] for h in range(HEADS)] + [delta[h : h + 1, :] for h in range(HEADS)]
    rest = jnp.concatenate(line, axis=1)
    parts = []
    for _ in range(3):
        low = rest.astype(bf16).astype(f32)
        parts.append(low)
        rest = rest - low
    parts.append(jnp.zeros((5, 2 * WIDE), f32))
    msg_ref[TOK:, :] = jnp.concatenate(parts, axis=0).astype(bf16)


def nt(left, right):
    return lax.dot_general(left, right, (((1,), (1,)), ((), ())), preferred_element_type=f32)


def nn(left, right):
    return lax.dot_general(left, right, (((1,), (0,)), ((), ())), preferred_element_type=f32)


def tile_kernel(cfg, *refs):
    it = iter(refs)

    def take(n):
        return [next(it) for _ in range(n)]

    start, count, s, finals, raws, old_units, has_acc, spread_out = cfg
    tab = next(it)
    msgs = take(count)
    kv, kcode, qlim = take(3)
    oldq = next(it) if old_units else None
    old = next(it) if has_acc else None
    gqs = take(len(finals))
    rawq = next(it) if raws else None
    out = next(it)
    qs, ds, lse, delta, ks, kt, kc, gq, work = take(9)
    acc = next(it) if spread_out else out
    base = 2 * start
    units = 2 * count
    chunks = KUNITS // GROUP
    filled = jnp.int32(0)
    for u in range(units):
        for c in range(chunks):
            work[filled] = c * units + u
            active = c * GROUP < tab[2 * KUNITS + s * QUNITS + base + u, 0]
            filled = filled + active.astype(jnp.int32)
    rounds = (filled + PAR - 1) // PAR
    for a, m in enumerate(msgs):
        meta = m[TOK : TOK + 8, :].astype(f32)
        meta = meta[0:1] + meta[1:2] + meta[2:3]
        for half in range(2):
            u = 2 * a + half
            rows = slice(half * UNIT, (half + 1) * UNIT)
            for h in range(HEADS):
                dst = slice(u * ROWS + h * UNIT, u * ROWS + (h + 1) * UNIT)
                qs[dst, :] = m[rows, h * DIM : (h + 1) * DIM]
                ds[dst, :] = m[rows, WIDE + h * DIM : WIDE + (h + 1) * DIM]
            for ref, first in ((lse, 0), (delta, WIDE)):
                cuts = [first + h * TOK + half * UNIT for h in range(HEADS)]
                ref[u] = jnp.concatenate([meta[:, c : c + UNIT] for c in cuts], axis=1)
    gq[...] = jnp.zeros_like(gq)
    if oldq is not None:
        gq[:old_units] = oldq[...]
    acc[...] = jnp.zeros_like(acc) if old is None else old[...]
    spots = []
    for b in range(NY):
        row = kcode[s * NY + b : s * NY + b + 1, :]
        wide = jnp.broadcast_to(row, (TOK, TOK)).T
        for half in range(2):
            i = half * NY + b
            spot = pl.multiple_of(tab[s * KUNITS + i, 0] * UNIT, UNIT)
            nat = slice(b * TOK + half * UNIT, b * TOK + (half + 1) * UNIT)
            spots.append((nat, spot))
            ks[pl.ds(spot, UNIT), :] = kv[nat, :]
            kc[pl.ds(spot, UNIT), :] = wide[half * UNIT : (half + 1) * UNIT]
    span = GROUP * UNIT
    for c in range(chunks):
        kt[c] = ks[c * span : (c + 1) * span, :DIM].astype(f32).T.astype(bf16)
    score_scale = DIM ** (-0.5)

    def item(index):
        code = jnp.where(index < filled, work[jnp.minimum(index, filled - 1)], 0)
        u = code % units
        c = code // units
        spot = pl.ds(pl.multiple_of(c * span, span), span)
        keys, vals = ks[spot, :DIM], ks[spot, DIM:]
        at = pl.ds(pl.multiple_of(u * ROWS, ROWS), ROWS)
        q, d = qs[at, :], ds[at, :]
        probs = jnp.exp(nt(keys, q) * score_scale - lse[u])
        kcodes = kc[spot, :]
        mod, pos = kcodes & 3, kcodes >> 2
        lim = jnp.where(index < filled, qlim[base + u], -1)
        bands = []
        for cut in (slice(0, DIM), slice(DIM, ROWS)):
            bound = jnp.where(mod == 0, lim[0:1, cut], jnp.where(mod == 1, lim[1:2, cut], lim[2:3, cut]))
            bands.append(jnp.where(pos <= bound, probs[:, cut], 0.0))
        probs = jnp.concatenate(bands, axis=1)
        grads = probs * (nt(vals, d) - delta[u])
        plow = probs.astype(bf16)
        glow = grads.astype(bf16)
        acc[spot, DIM:] += nn(plow, d)
        acc[spot, :DIM] += nn(glow, q)
        gq[u] += nn(kt[c], glow)

    def body(r, _):
        for j in range(PAR):
            item(r * PAR + j)
        return 0

    lax.fori_loop(0, rounds, body, 0)
    if spread_out:
        for nat, spot in spots:
            out[nat, :] = acc[pl.ds(spot, UNIT), :].astype(out.dtype)
    if rawq is not None:
        rawq[...] = gq[raws[0] : raws[1]]
    for (a, _), g in zip(finals, gqs):
        for half in range(2):
            rows = slice(half * UNIT, (half + 1) * UNIT)
            whole = gq[2 * a + half].T
            for h in range(HEADS):
                part = whole[h * UNIT : (h + 1) * UNIT, :]
                g[rows, h * DIM : (h + 1) * DIM] = part.astype(g.dtype)


def in_vmem(value):
    return pltpu.with_memory_space_constraint(value, pltpu.VMEM)


def tile(tab, start, msgs, kv, kcode, qlim, s, finals=(), raws=None, oldq=None, old=None, out_type=None):
    count = len(msgs)
    units = 2 * count
    keys = KUNITS * UNIT
    smem = pl.BlockSpec(memory_space=pltpu.SMEM)
    vmem = pl.BlockSpec(memory_space=pltpu.VMEM)
    arrays = [*msgs, kv, kcode, qlim] + [v for v in (oldq, old) if v is not None]
    outs = [pltpu.VMEM((TOK, WIDE), t) for _, t in finals]
    if raws:
        outs.append(pltpu.VMEM((raws[1] - raws[0], DIM, ROWS), f32))
    outs.append(pltpu.VMEM((keys, 2 * DIM), out_type or f32))
    scratch = [
        pltpu.VMEM((units * ROWS, DIM), bf16),
        pltpu.VMEM((units * ROWS, DIM), bf16),
        pltpu.VMEM((units, 1, ROWS), f32),
        pltpu.VMEM((units, 1, ROWS), f32),
        pltpu.VMEM((keys, 2 * DIM), bf16),
        pltpu.VMEM((KUNITS // GROUP, DIM, GROUP * UNIT), bf16),
        pltpu.VMEM((keys, DIM), jnp.int32),
        pltpu.VMEM((units, DIM, ROWS), f32),
        pltpu.SMEM((units * (KUNITS // GROUP) + 1,), jnp.int32),
    ]
    if out_type:
        scratch.append(pltpu.VMEM((keys, 2 * DIM), f32))
    cfg = (
        start, count, s, finals, raws, 0 if oldq is None else oldq.shape[0], old is not None, out_type is not None
    )

    def body(*refs):
        tile_kernel(cfg, *refs)

    return pl.pallas_call(
        body,
        in_specs=[smem] + [vmem] * len(arrays),
        out_specs=[vmem] * len(outs),
        out_shape=outs,
        scratch_shapes=scratch,
        compiler_params=pltpu.CompilerParams(vmem_limit_bytes=20 << 20),
    )(tab, *[in_vmem(v) for v in arrays])


def finish_kernel(parts, key_ref, value_ref):
    total = jnp.sum(parts[...].astype(f32), axis=0)
    key_ref[...] = (total[:, :DIM] * DIM ** (-0.5)).astype(bf16)
    value_ref[...] = total[:, DIM:].astype(bf16)


def unit_low(value, fold, fill):
    lane = lax.broadcasted_iota(jnp.int32, value.shape, 1)
    first = fold(jnp.where(lane < UNIT, value, fill), axis=1, keepdims=True)
    second = fold(jnp.where(lane < UNIT, fill, value), axis=1, keepdims=True)
    return first, second


def plan_kernel(table, position, modality, tab, kcode, qlim, rows, sems):
    y, zlo, core, x, zhh, zhl = (lax.axis_index(a) for a in AXES)

    def line(y, zlo, core, zhl):
        return ((((y * 2 + zlo) * 2 + core) * 4 + x) * 2 + zhh) * 2 + zhl

    lines = [line(b, zlo, core ^ s, zhl) for s in range(2) for b in range(NY)]
    lines += [line(y, zlo ^ (mask >> 1), core, zhl ^ (mask & 1)) for mask in MASKS]
    moves = []
    for i, at in enumerate(lines):
        for j, ref in enumerate((position, modality)):
            moves.append(pltpu.make_async_copy(ref.at[at], rows.at[j, i], sems.at[j, i]))
    for move in moves:
        move.start()
    for move in moves:
        move.wait()
    pos = jnp.concatenate([rows[0, i] for i in range(len(lines))], axis=0)
    mod = jnp.concatenate([rows[1, i] for i in range(len(lines))], axis=0)
    keys = 2 * NY
    kcode[...] = pos[:keys] * 4 + mod[:keys]
    low = unit_low(pos[:keys], jnp.min, 1 << 20)
    high = unit_low(pos[keys:], jnp.max, -1)
    qlast = jnp.concatenate(
        [high[half][a : a + 1] for a in range(NZ) for half in range(2)], axis=0
    )
    qlast = jnp.broadcast_to(qlast, (QUNITS, TOK)) >> 6
    lane = lax.broadcasted_iota(jnp.int32, (KUNITS, TOK), 1)
    index = lax.broadcasted_iota(jnp.int32, (KUNITS, TOK), 0)
    for s in range(2):
        part = slice(s * NY, (s + 1) * NY)
        column = jnp.broadcast_to(jnp.concatenate([low[0][part], low[1][part]], axis=0), (KUNITS, TOK))
        square = jnp.concatenate([column, jnp.zeros((TOK - KUNITS, TOK), jnp.int32)], axis=0).T
        across = square[:KUNITS]
        before = ((across < column) | ((across == column) & (lane < index))) & (lane < KUNITS)
        rank = jnp.sum(before.astype(jnp.int32), axis=1, keepdims=True)
        tab[s * KUNITS : (s + 1) * KUNITS, :] = jnp.broadcast_to(rank, (KUNITS, TOK))
        seen = ((across[:QUNITS] >> 6) <= qlast) & (lane[:QUNITS] < KUNITS)
        need = jnp.sum(seen.astype(jnp.int32), axis=1, keepdims=True)
        at = 2 * KUNITS + s * QUNITS
        tab[at : at + QUNITS, :] = jnp.broadcast_to(need, (QUNITS, TOK))
    qpos, qmod = pos[keys:], mod[keys:]
    for m in range(3):
        bid = jnp.where(qmod == 0, table[0, m], jnp.where(qmod == 1, table[1, m], table[2, m]))
        lim = jnp.where(bid == 1, qpos | (UNIT - 1), qpos)
        for a in range(NZ):
            for half in range(2):
                cut = lim[a : a + 1, half * UNIT : (half + 1) * UNIT]
                qlim[2 * a + half, m : m + 1, :] = jnp.concatenate([cut] * HEADS, axis=1)


def plan(position, modality, table):
    hbm = pl.BlockSpec(memory_space=pltpu.HBM)
    vmem = pl.BlockSpec(memory_space=pltpu.VMEM)
    count = 2 * NY + NZ
    lines = position.shape[0] // TOK
    return pl.pallas_call(
        plan_kernel,
        in_specs=[pl.BlockSpec(memory_space=pltpu.SMEM), hbm, hbm],
        out_specs=[vmem] * 3,
        out_shape=[
            jax.ShapeDtypeStruct((2 * KUNITS + 2 * QUNITS, TOK), jnp.int32),
            pltpu.VMEM((2 * NY, TOK), jnp.int32),
            pltpu.VMEM((QUNITS, 3, ROWS), jnp.int32),
        ],
        scratch_shapes=[
            pltpu.VMEM((2, count, 1, TOK), jnp.int32),
            pltpu.SemaphoreType.DMA((2, count)),
        ],
        compiler_params=pltpu.CompilerParams(vmem_limit_bytes=8 << 20),
        name="plan",
    )(
        table,
        pltpu.with_memory_space_constraint(position.reshape(lines, 1, TOK), pltpu.HBM),
        pltpu.with_memory_space_constraint(modality.reshape(lines, 1, TOK), pltpu.HBM),
    )


def shards(queries, grad_out, attn_out, key_states, value_states, log_norm, position, modality, table):
    def along_z(value, mask):
        return lax.ppermute(value, ("zlo", "zhl"), [(i, i ^ mask) for i in range(NZ)])

    def other_core(value):
        return lax.ppermute(value, "core", [(0, 1), (1, 0)])

    def over_y(value):
        return lax.all_to_all(value, "y", 0, 0)

    pair = jnp.concatenate([key_states, value_states], axis=1)
    copies = jnp.broadcast_to(pair[None], (NY, TOK, 2 * DIM))
    msg = pl.pallas_call(
        pack_kernel, out_shape=pltpu.VMEM((TOK + 8, 2 * WIDE), bf16), compiler_params=pltpu.CompilerParams(vmem_limit_bytes=8 << 20), name="pack"
    )(queries, grad_out, attn_out, log_norm.T)
    kvo = over_y(copies).reshape(NY * TOK, 2 * DIM)
    far = along_z(msg, 1)
    near = along_z(msg, 2)
    tab, kcode, qlim = plan(position, modality, table)
    kvx = other_core(kvo)
    last = along_z(far, 2)
    raw_near, old_own = tile(tab, 0, (msg, near), kvo, kcode, qlim, 0, raws=(0, 4))
    own_q, near_q, old_oth = tile(tab, 0, (msg, near), kvx, kcode, qlim, 1, ((0, f32), (1, bf16)), None, raw_near)
    raw_far, gkvx = tile(tab, 2, (far, last), kvx, kcode, qlim, 1, (), (0, 4), None, old_oth, bf16)
    got = other_core(gkvx)
    far_q, last_q, gkvo = tile(
        tab, 2, (far, last), kvo, kcode, qlim, 0, ((0, bf16), (1, bf16)), None, raw_far, old_own, f32
    )
    paired = (gkvo + got.astype(f32)).astype(bf16).reshape(NY, TOK, 2 * DIM)
    summed = over_y(paired)
    narrow = jax.ShapeDtypeStruct((TOK, DIM), bf16)
    grad_key, grad_value = pl.pallas_call(
        finish_kernel, out_shape=[narrow] * 2, compiler_params=pltpu.CompilerParams(vmem_limit_bytes=8 << 20), name="finish"
    )(in_vmem(summed))
    back = [along_z(g, mask) for g, mask in zip((near_q, far_q, last_q), MASKS[1:])]
    grad_q = (own_q + back[0].astype(f32) + back[1].astype(f32) + back[2].astype(f32)) * DIM ** (-0.5)
    return grad_q.astype(bf16), grad_key, grad_value


def solution(mesh):
    fine = Mesh(mesh.devices.reshape(8, 2, 2, 4, 2, 2), AXES)
    tokens = P(AXES, None)

    return jax.shard_map(
        shards,
        mesh=fine,
        in_specs=(tokens,) * 6 + (P(), P(), P()),
        out_specs=(tokens,) * 3,
        check_vma=False,
    )
```

```python
import jax
import jax.numpy as jnp
from jax import lax
from jax.experimental import pallas as pl
from jax.experimental.pallas import tpu as pltpu
from jax.sharding import Mesh, PartitionSpec as P

UNIT = 64
TOK = 128
HEADS = 4
DIM = 128
WIDE = HEADS * DIM
NZ = 4
NY = 8
QUNITS = 2 * NZ
KUNITS = NY * TOK // UNIT
GROUP = 8
PAR = 3
MASKS = (0, 2, 1, 3)
ROWS = HEADS * UNIT
AXES = ("y", "zlo", "core", "x", "zhh", "zhl")
bf16 = jnp.bfloat16
f32 = jnp.float32


def pack_kernel(q_ref, d_ref, o_ref, lse_ref, msg_ref):
    msg_ref[:TOK, :WIDE] = q_ref[...]
    msg_ref[:TOK, WIDE:] = d_ref[...]
    lane = lax.broadcasted_iota(jnp.int32, (TOK, DIM), 1)
    delta = jnp.zeros((TOK, DIM), f32)
    for h in range(HEADS):
        cut = slice(h * DIM, (h + 1) * DIM)
        column = jnp.sum(d_ref[:, cut].astype(f32) * o_ref[:, cut].astype(f32), axis=1, keepdims=True)
        delta = jnp.where(lane == h, column, delta)
    delta = delta.T
    line = [lse_ref[h : h + 1, :] for h in range(HEADS)] + [delta[h : h + 1, :] for h in range(HEADS)]
    rest = jnp.concatenate(line, axis=1)
    parts = []
    for _ in range(3):
        low = rest.astype(bf16).astype(f32)
        parts.append(low)
        rest = rest - low
    parts.append(jnp.zeros((5, 2 * WIDE), f32))
    msg_ref[TOK:, :] = jnp.concatenate(parts, axis=0).astype(bf16)


def nt(left, right):
    return lax.dot_general(left, right, (((1,), (1,)), ((), ())), preferred_element_type=f32)


def nn(left, right):
    return lax.dot_general(left, right, (((1,), (0,)), ((), ())), preferred_element_type=f32)


def tile_kernel(cfg, *refs):
    it = iter(refs)

    def take(n):
        return [next(it) for _ in range(n)]

    start, count, sets, given, finals, raws, old_units, export_q = cfg
    q_given, k_given = given
    spread_out = k_given
    tab = next(it)
    msgs = [] if q_given else take(count)
    kvs = [] if k_given else take(len(sets))
    kcode = None if k_given else next(it)
    qlim = next(it)
    q_parts = take(4) if q_given else None
    k_parts = take(3) if k_given else None
    oldq = next(it) if old_units else None
    old = next(it) if k_given else None
    gqs = take(len(finals))
    rawq = next(it) if raws else None
    out = next(it)
    if q_parts is None and export_q:
        q_parts = take(4)
    if k_parts is None:
        k_parts = take(3)
    if q_parts is None:
        q_parts = take(4)
    gq, work = take(2)
    acc = next(it) if spread_out else out
    qs, ds, lse, delta = q_parts
    ks, kt, kc = k_parts
    base = 2 * start
    units = 2 * count
    chunks = KUNITS // GROUP
    keys = KUNITS * UNIT
    span = GROUP * UNIT
    chunk0 = sets[0] * chunks
    filled = jnp.int32(0)
    for which, s in enumerate(sets):
        for u in range(units):
            for c in range(chunks):
                work[filled] = (which * chunks + c) * units + u
                active = c * GROUP < tab[2 + s, base + u]
                filled = filled + active.astype(jnp.int32)
    rounds = (filled + PAR - 1) // PAR
    for a, m in enumerate(msgs):
        meta = m[TOK : TOK + 8, :].astype(f32)
        meta = meta[0:1] + meta[1:2] + meta[2:3]
        for half in range(2):
            u = 2 * a + half
            rows = slice(half * UNIT, (half + 1) * UNIT)
            for h in range(HEADS):
                dst = slice(u * ROWS + h * UNIT, u * ROWS + (h + 1) * UNIT)
                qs[dst, :] = m[rows, h * DIM : (h + 1) * DIM]
                ds[dst, :] = m[rows, WIDE + h * DIM : WIDE + (h + 1) * DIM]
            for ref, first in ((lse, 0), (delta, WIDE)):
                cuts = [first + h * TOK + half * UNIT for h in range(HEADS)]
                ref[u] = jnp.concatenate([meta[:, c : c + UNIT] for c in cuts], axis=1)
    gq[...] = jnp.zeros_like(gq) if oldq is None else oldq[...]
    if old is None:
        acc[...] = jnp.zeros_like(acc)
    else:
        acc[...] = old[sets[0] * keys : (sets[0] + 1) * keys, :]
    spots = []
    for which, s in enumerate(sets):
        for b in range(NY):
            if not k_given:
                row = kcode[s * NY + b : s * NY + b + 1, :]
                wide = jnp.broadcast_to(row, (TOK, TOK)).T
            for half in range(2):
                at = tab[s, half * NY + b] + which * KUNITS
                spot = pl.multiple_of(at * UNIT, UNIT)
                nat = slice(b * TOK + half * UNIT, b * TOK + (half + 1) * UNIT)
                spots.append((nat, spot))
                if not k_given:
                    ks[pl.ds(spot, UNIT), :] = kvs[which][nat, :]
                    kc[pl.ds(spot, UNIT), :] = wide[half * UNIT : (half + 1) * UNIT]
    if not k_given:
        for c in range(chunks * len(sets)):
            kt[c] = ks[c * span : (c + 1) * span, :DIM].astype(f32).T.astype(bf16)
    score_scale = DIM ** (-0.5)

    def item(index):
        code = jnp.where(index < filled, work[jnp.minimum(index, filled - 1)], 0)
        u = code % units
        c = code // units
        spot = pl.ds(pl.multiple_of(c * span, span), span)
        where_ = pl.ds(pl.multiple_of((chunk0 + c) * span, span), span)
        keys, vals = ks[where_, :DIM], ks[where_, DIM:]
        at = pl.ds(pl.multiple_of(u * ROWS, ROWS), ROWS)
        q, d = qs[at, :], ds[at, :]
        probs = jnp.exp(nt(keys, q) * score_scale - lse[u])
        kcodes = kc[where_, :]
        mod, pos = kcodes & 3, kcodes >> 2
        lim = jnp.where(index < filled, qlim[base + u], -1)
        bands = []
        for cut in (slice(0, DIM), slice(DIM, ROWS)):
            bound = jnp.where(mod == 0, lim[0:1, cut], jnp.where(mod == 1, lim[1:2, cut], lim[2:3, cut]))
            bands.append(jnp.where(pos <= bound, probs[:, cut], 0.0))
        probs = jnp.concatenate(bands, axis=1)
        grads = probs * (nt(vals, d) - delta[u])
        plow = probs.astype(bf16)
        glow = grads.astype(bf16)
        acc[spot, DIM:] += nn(plow, d)
        acc[spot, :DIM] += nn(glow, q)
        gq[u] += nn(kt[chunk0 + c], glow)

    def body(r, _):
        for j in range(PAR):
            item(r * PAR + j)
        return 0

    lax.fori_loop(0, rounds, body, 0)
    if spread_out:
        for nat, spot in spots:
            out[nat, :] = acc[pl.ds(spot, UNIT), :].astype(out.dtype)
    if rawq is not None:
        rawq[...] = gq[raws[0] : raws[1]]
    for (a, _), g in zip(finals, gqs):
        for half in range(2):
            rows = slice(half * UNIT, (half + 1) * UNIT)
            whole = gq[2 * a + half].T
            for h in range(HEADS):
                part = whole[h * UNIT : (h + 1) * UNIT, :]
                g[rows, h * DIM : (h + 1) * DIM] = part.astype(g.dtype)


def in_vmem(value):
    return pltpu.with_memory_space_constraint(value, pltpu.VMEM)


def tile(tab, start, sets, qlim, msgs=(), kvs=(), kcode=None, q_parts=None, k_parts=None, finals=(),
         raws=None, oldq=None, old=None, out_type=f32, export_q=False):
    count = q_parts[2].shape[0] // 2 if q_parts is not None else len(msgs)
    units = 2 * count
    keys = len(sets) * KUNITS * UNIT
    smem = pl.BlockSpec(memory_space=pltpu.SMEM)
    vmem = pl.BlockSpec(memory_space=pltpu.VMEM)
    arrays = [*msgs, *kvs] + ([] if kcode is None else [kcode]) + [qlim]
    arrays += [*(q_parts or ()), *(k_parts or ())] + [v for v in (oldq, old) if v is not None]
    q_shapes = [
        pltpu.VMEM((units * ROWS, DIM), bf16),
        pltpu.VMEM((units * ROWS, DIM), bf16),
        pltpu.VMEM((units, 1, ROWS), f32),
        pltpu.VMEM((units, 1, ROWS), f32),
    ]
    k_shapes = [
        pltpu.VMEM((keys, 2 * DIM), bf16),
        pltpu.VMEM((keys // (GROUP * UNIT), DIM, GROUP * UNIT), bf16),
        pltpu.VMEM((keys, DIM), jnp.int32),
    ]
    outs = [pltpu.VMEM((TOK, WIDE), t) for _, t in finals]
    if raws:
        outs.append(pltpu.VMEM((raws[1] - raws[0], DIM, ROWS), f32))
    outs.append(pltpu.VMEM((keys, 2 * DIM), out_type))
    if q_parts is None and export_q:
        outs += q_shapes
    if k_parts is None:
        outs += k_shapes
    scratch = [
        pltpu.VMEM((units, DIM, ROWS), f32),
        pltpu.SMEM((units * len(sets) * (KUNITS // GROUP) + 1,), jnp.int32),
    ]
    if q_parts is None and not export_q:
        scratch = q_shapes + scratch
    if k_parts is not None:
        scratch.append(pltpu.VMEM((keys, 2 * DIM), f32))
    given = (q_parts is not None, k_parts is not None)
    cfg = (start, count, sets, given, finals, raws, 0 if oldq is None else units, export_q)

    def body(*refs):
        tile_kernel(cfg, *refs)

    return pl.pallas_call(
        body,
        in_specs=[smem] + [vmem] * len(arrays),
        out_specs=[vmem] * len(outs),
        out_shape=outs,
        scratch_shapes=scratch,
        compiler_params=pltpu.CompilerParams(vmem_limit_bytes=20 << 20),
    )(tab, *[in_vmem(v) for v in arrays])


def finish_kernel(parts, key_ref, value_ref):
    total = jnp.sum(parts[...].astype(f32), axis=0)
    key_ref[...] = (total[:, :DIM] * DIM ** (-0.5)).astype(bf16)
    value_ref[...] = total[:, DIM:].astype(bf16)


def unit_low(value, fold, fill):
    lane = lax.broadcasted_iota(jnp.int32, value.shape, 1)
    first = fold(jnp.where(lane < UNIT, value, fill), axis=1, keepdims=True)
    second = fold(jnp.where(lane < UNIT, fill, value), axis=1, keepdims=True)
    return first, second


def plan_kernel(table, position, modality, tab, kcode, qlim, rows, sems):
    y, zlo, core, x, zhh, zhl = (lax.axis_index(a) for a in AXES)

    def line(y, zlo, core, zhl):
        return ((((y * 2 + zlo) * 2 + core) * 4 + x) * 2 + zhh) * 2 + zhl

    lines = [line(b, zlo, core ^ s, zhl) for s in range(2) for b in range(NY)]
    lines += [line(y, zlo ^ (mask >> 1), core, zhl ^ (mask & 1)) for mask in MASKS]
    moves = []
    for i, at in enumerate(lines):
        for j, ref in enumerate((position, modality)):
            moves.append(pltpu.make_async_copy(ref.at[at], rows.at[j, i], sems.at[j, i]))
    for move in moves:
        move.start()
    for move in moves:
        move.wait()
    pos = jnp.concatenate([rows[0, i] for i in range(len(lines))], axis=0)
    mod = jnp.concatenate([rows[1, i] for i in range(len(lines))], axis=0)
    keys = 2 * NY
    kcode[...] = pos[:keys] * 4 + mod[:keys]
    low = unit_low(pos[:keys], jnp.min, 1 << 20)
    high = unit_low(pos[keys:], jnp.max, -1)
    qlast = jnp.concatenate(
        [high[half][a : a + 1] for a in range(NZ) for half in range(2)], axis=0
    )
    qlast = jnp.concatenate([qlast, jnp.zeros((TOK - QUNITS, 1), jnp.int32)], axis=0)
    qlast = jnp.broadcast_to(qlast, (TOK, TOK)).T[:KUNITS] >> 6
    lane = lax.broadcasted_iota(jnp.int32, (KUNITS, TOK), 1)
    index = lax.broadcasted_iota(jnp.int32, (KUNITS, TOK), 0)
    for s in range(2):
        part = slice(s * NY, (s + 1) * NY)
        column = jnp.broadcast_to(jnp.concatenate([low[0][part], low[1][part]], axis=0), (KUNITS, TOK))
        square = jnp.concatenate([column, jnp.zeros((TOK - KUNITS, TOK), jnp.int32)], axis=0).T
        across = square[:KUNITS]
        before = (column < across) | ((column == across) & (index < lane))
        tab[s : s + 1, :] = jnp.sum(before.astype(jnp.int32), axis=0, keepdims=True)
        seen = (column >> 6) <= qlast
        tab[2 + s : 3 + s, :] = jnp.sum(seen.astype(jnp.int32), axis=0, keepdims=True)
    qpos, qmod = pos[keys:], mod[keys:]
    for m in range(3):
        bid = jnp.where(qmod == 0, table[0, m], jnp.where(qmod == 1, table[1, m], table[2, m]))
        lim = jnp.where(bid == 1, qpos | (UNIT - 1), qpos)
        for a in range(NZ):
            for half in range(2):
                cut = lim[a : a + 1, half * UNIT : (half + 1) * UNIT]
                qlim[2 * a + half, m : m + 1, :] = jnp.concatenate([cut] * HEADS, axis=1)


def plan(position, modality, table):
    hbm = pl.BlockSpec(memory_space=pltpu.HBM)
    vmem = pl.BlockSpec(memory_space=pltpu.VMEM)
    count = 2 * NY + NZ
    lines = position.shape[0] // TOK
    return pl.pallas_call(
        plan_kernel,
        in_specs=[pl.BlockSpec(memory_space=pltpu.SMEM), hbm, hbm],
        out_specs=[vmem] * 3,
        out_shape=[
            jax.ShapeDtypeStruct((4, TOK), jnp.int32),
            pltpu.VMEM((2 * NY, TOK), jnp.int32),
            pltpu.VMEM((QUNITS, 3, ROWS), jnp.int32),
        ],
        scratch_shapes=[
            pltpu.VMEM((2, count, 1, TOK), jnp.int32),
            pltpu.SemaphoreType.DMA((2, count)),
        ],
        compiler_params=pltpu.CompilerParams(vmem_limit_bytes=8 << 20),
        name="plan",
    )(
        table,
        pltpu.with_memory_space_constraint(position.reshape(lines, 1, TOK), pltpu.HBM),
        pltpu.with_memory_space_constraint(modality.reshape(lines, 1, TOK), pltpu.HBM),
    )


def shards(queries, grad_out, attn_out, key_states, value_states, log_norm, position, modality, table):
    def along_z(value, mask):
        return lax.ppermute(value, ("zlo", "zhl"), [(i, i ^ mask) for i in range(NZ)])

    def other_core(value):
        return lax.ppermute(value, "core", [(0, 1), (1, 0)])

    def over_y(value):
        return lax.all_to_all(value, "y", 0, 0)

    pair = jnp.concatenate([key_states, value_states], axis=1)
    copies = jnp.broadcast_to(pair[None], (NY, TOK, 2 * DIM))
    msg = pl.pallas_call(
        pack_kernel, out_shape=pltpu.VMEM((TOK + 8, 2 * WIDE), bf16), compiler_params=pltpu.CompilerParams(vmem_limit_bytes=8 << 20), name="pack"
    )(queries, grad_out, attn_out, log_norm.T)
    kvo = over_y(copies).reshape(NY * TOK, 2 * DIM)
    far = along_z(msg, 1)
    near = along_z(msg, 2)
    tab, kcode, qlim = plan(position, modality, table)
    kvx = other_core(kvo)
    last = along_z(far, 2)
    own_q, near_q, old, *k_parts = tile(
        tab, 0, (0, 1), qlim, (msg, near), (kvo, kvx), kcode, finals=((0, f32), (1, bf16))
    )
    raw_far, gkvx, *q_parts = tile(
        tab, 2, (1,), qlim, (far, last), k_parts=k_parts, raws=(0, 4), old=old, out_type=bf16,
        export_q=True,
    )
    got = other_core(gkvx)
    far_q, last_q, gkvo = tile(
        tab, 2, (0,), qlim, q_parts=q_parts, k_parts=k_parts, finals=((0, bf16), (1, bf16)),
        oldq=raw_far, old=old,
    )
    paired = (gkvo + got.astype(f32)).astype(bf16).reshape(NY, TOK, 2 * DIM)
    summed = over_y(paired)
    narrow = jax.ShapeDtypeStruct((TOK, DIM), bf16)
    grad_key, grad_value = pl.pallas_call(
        finish_kernel, out_shape=[narrow] * 2, compiler_params=pltpu.CompilerParams(vmem_limit_bytes=8 << 20), name="finish"
    )(in_vmem(summed))
    back = [along_z(g, mask) for g, mask in zip((near_q, far_q, last_q), MASKS[1:])]
    grad_q = (own_q + back[0].astype(f32) + back[1].astype(f32) + back[2].astype(f32)) * DIM ** (-0.5)
    return grad_q.astype(bf16), grad_key, grad_value


def solution(mesh):
    fine = Mesh(mesh.devices.reshape(8, 2, 2, 4, 2, 2), AXES)
    tokens = P(AXES, None)

    return jax.shard_map(
        shards,
        mesh=fine,
        in_specs=(tokens,) * 6 + (P(), P(), P()),
        out_specs=(tokens,) * 3,
        check_vma=False,
    )
```

```python
import jax
import jax.numpy as jnp
from jax import lax
from jax.experimental import pallas as pl
from jax.experimental.pallas import tpu as pltpu
from jax.sharding import Mesh, PartitionSpec as P

UNIT = 64
TOK = 128
HEADS = 4
DIM = 128
WIDE = HEADS * DIM
NZ = 4
NY = 8
QUNITS = 2 * NZ
KUNITS = NY * TOK // UNIT
GROUP = 8
PAR = 3
MASKS = (0, 2, 1, 3)
ROWS = HEADS * UNIT
AXES = ("y", "zlo", "core", "x", "zhh", "zhl")
bf16 = jnp.bfloat16
f32 = jnp.float32


def pack_kernel(q_ref, d_ref, o_ref, lse_ref, msg_ref):
    msg_ref[:TOK, :WIDE] = q_ref[...]
    msg_ref[:TOK, WIDE:] = d_ref[...]
    lane = lax.broadcasted_iota(jnp.int32, (TOK, DIM), 1)
    delta = jnp.zeros((TOK, DIM), f32)
    for h in range(HEADS):
        cut = slice(h * DIM, (h + 1) * DIM)
        column = jnp.sum(d_ref[:, cut].astype(f32) * o_ref[:, cut].astype(f32), axis=1, keepdims=True)
        delta = jnp.where(lane == h, column, delta)
    delta = delta.T
    line = [lse_ref[h : h + 1, :] for h in range(HEADS)] + [delta[h : h + 1, :] for h in range(HEADS)]
    rest = jnp.concatenate(line, axis=1)
    parts = []
    for _ in range(3):
        low = rest.astype(bf16).astype(f32)
        parts.append(low)
        rest = rest - low
    parts.append(jnp.zeros((5, 2 * WIDE), f32))
    msg_ref[TOK:, :] = jnp.concatenate(parts, axis=0).astype(bf16)


def nt(left, right):
    return lax.dot_general(left, right, (((1,), (1,)), ((), ())), preferred_element_type=f32)


def nn(left, right):
    return lax.dot_general(left, right, (((1,), (0,)), ((), ())), preferred_element_type=f32)


def tile_kernel(cfg, *refs):
    it = iter(refs)

    def take(n):
        return [next(it) for _ in range(n)]

    start, count, sets, given, finals, raws, old_units, export_q = cfg
    q_given, k_given = given
    spread_out = k_given
    tab = next(it)
    msgs = [] if q_given else take(count)
    kvs = [] if k_given else take(len(sets))
    kcode = None if k_given else next(it)
    qlim = next(it)
    q_parts = take(4) if q_given else None
    k_parts = take(3) if k_given else None
    oldq = next(it) if old_units else None
    old = next(it) if k_given else None
    gqs = take(len(finals))
    rawq = next(it) if raws else None
    out = next(it)
    if q_parts is None and export_q:
        q_parts = take(4)
    if k_parts is None:
        k_parts = take(3)
    if q_parts is None:
        q_parts = take(4)
    gq, work = take(2)
    acc = next(it) if spread_out else out
    qs, ds, lse, delta = q_parts
    ks, kt, kc = k_parts
    base = 2 * start
    units = 2 * count
    chunks = KUNITS // GROUP
    keys = KUNITS * UNIT
    span = GROUP * UNIT
    chunk0 = sets[0] * chunks
    filled = jnp.int32(0)
    for which, s in enumerate(sets):
        for u in range(units):
            for c in range(chunks):
                work[filled] = (which * chunks + c) * units + u
                active = c * GROUP < tab[2 + s, base + u]
                filled = filled + active.astype(jnp.int32)
    rounds = (filled + PAR - 1) // PAR
    for a, m in enumerate(msgs):
        meta = m[TOK : TOK + 8, :].astype(f32)
        meta = meta[0:1] + meta[1:2] + meta[2:3]
        for half in range(2):
            u = 2 * a + half
            rows = slice(half * UNIT, (half + 1) * UNIT)
            for h in range(HEADS):
                dst = slice(u * ROWS + h * UNIT, u * ROWS + (h + 1) * UNIT)
                qs[dst, :] = m[rows, h * DIM : (h + 1) * DIM]
                ds[dst, :] = m[rows, WIDE + h * DIM : WIDE + (h + 1) * DIM]
            for ref, first in ((lse, 0), (delta, WIDE)):
                cuts = [first + h * TOK + half * UNIT for h in range(HEADS)]
                ref[u] = jnp.concatenate([meta[:, c : c + UNIT] for c in cuts], axis=1)
    gq[...] = jnp.zeros_like(gq) if oldq is None else oldq[...]
    if old is None:
        acc[...] = jnp.zeros_like(acc)
    else:
        acc[...] = old[sets[0] * keys : (sets[0] + 1) * keys, :]
    spots = []
    for which, s in enumerate(sets):
        for b in range(NY):
            if not k_given:
                row = kcode[s * NY + b : s * NY + b + 1, :]
                wide = jnp.broadcast_to(row, (TOK, TOK)).T
            for half in range(2):
                at = tab[s, half * NY + b] + which * KUNITS
                spot = pl.multiple_of(at * UNIT, UNIT)
                nat = slice(b * TOK + half * UNIT, b * TOK + (half + 1) * UNIT)
                spots.append((nat, spot))
                if not k_given:
                    ks[pl.ds(spot, UNIT), :] = kvs[which][nat, :]
                    kc[pl.ds(spot, UNIT), :] = wide[half * UNIT : (half + 1) * UNIT]
    if not k_given:
        for c in range(chunks * len(sets)):
            kt[c] = ks[c * span : (c + 1) * span, :DIM].astype(f32).T.astype(bf16)
    score_scale = DIM ** (-0.5)

    def item(index):
        code = jnp.where(index < filled, work[jnp.minimum(index, filled - 1)], 0)
        u = code % units
        c = code // units
        spot = pl.ds(pl.multiple_of(c * span, span), span)
        where_ = pl.ds(pl.multiple_of((chunk0 + c) * span, span), span)
        keys, vals = ks[where_, :DIM], ks[where_, DIM:]
        at = pl.ds(pl.multiple_of(u * ROWS, ROWS), ROWS)
        q, d = qs[at, :], ds[at, :]
        probs = jnp.exp(nt(keys, q) * score_scale - lse[u])
        kcodes = kc[where_, :]
        mod, pos = kcodes & 3, kcodes >> 2
        lim = jnp.where(index < filled, qlim[base + u], -1)
        bands = []
        for cut in (slice(0, DIM), slice(DIM, ROWS)):
            bound = jnp.where(mod == 0, lim[0:1, cut], jnp.where(mod == 1, lim[1:2, cut], lim[2:3, cut]))
            bands.append(jnp.where(pos <= bound, probs[:, cut], 0.0))
        probs = jnp.concatenate(bands, axis=1)
        grads = probs * (nt(vals, d) - delta[u])
        plow = probs.astype(bf16)
        glow = grads.astype(bf16)
        acc[spot, DIM:] += nn(plow, d)
        acc[spot, :DIM] += nn(glow, q)
        gq[u] += nn(kt[chunk0 + c], glow)

    def body(r, _):
        for j in range(PAR):
            item(r * PAR + j)
        return 0

    lax.fori_loop(0, rounds, body, 0)
    if spread_out:
        for nat, spot in spots:
            out[nat, :] = acc[pl.ds(spot, UNIT), :].astype(out.dtype)
    if rawq is not None:
        rawq[...] = gq[raws[0] : raws[1]]
    for (a, _), g in zip(finals, gqs):
        for half in range(2):
            rows = slice(half * UNIT, (half + 1) * UNIT)
            whole = gq[2 * a + half].T
            for h in range(HEADS):
                part = whole[h * UNIT : (h + 1) * UNIT, :]
                g[rows, h * DIM : (h + 1) * DIM] = part.astype(g.dtype)


def in_vmem(value):
    return pltpu.with_memory_space_constraint(value, pltpu.VMEM)


def tile(tab, start, sets, qlim, msgs=(), kvs=(), kcode=None, q_parts=None, k_parts=None, finals=(),
         raws=None, oldq=None, old=None, out_type=f32, export_q=False):
    count = q_parts[2].shape[0] // 2 if q_parts is not None else len(msgs)
    units = 2 * count
    keys = len(sets) * KUNITS * UNIT
    smem = pl.BlockSpec(memory_space=pltpu.SMEM)
    vmem = pl.BlockSpec(memory_space=pltpu.VMEM)
    arrays = [*msgs, *kvs] + ([] if kcode is None else [kcode]) + [qlim]
    arrays += [*(q_parts or ()), *(k_parts or ())] + [v for v in (oldq, old) if v is not None]
    q_shapes = [
        pltpu.VMEM((units * ROWS, DIM), bf16),
        pltpu.VMEM((units * ROWS, DIM), bf16),
        pltpu.VMEM((units, 1, ROWS), f32),
        pltpu.VMEM((units, 1, ROWS), f32),
    ]
    k_shapes = [
        pltpu.VMEM((keys, 2 * DIM), bf16),
        pltpu.VMEM((keys // (GROUP * UNIT), DIM, GROUP * UNIT), bf16),
        pltpu.VMEM((keys, DIM), jnp.int32),
    ]
    outs = [pltpu.VMEM((TOK, WIDE), t) for _, t in finals]
    if raws:
        outs.append(pltpu.VMEM((raws[1] - raws[0], DIM, ROWS), f32))
    outs.append(pltpu.VMEM((keys, 2 * DIM), out_type))
    if q_parts is None and export_q:
        outs += q_shapes
    if k_parts is None:
        outs += k_shapes
    scratch = [
        pltpu.VMEM((units, DIM, ROWS), f32),
        pltpu.SMEM((units * len(sets) * (KUNITS // GROUP) + 1,), jnp.int32),
    ]
    if q_parts is None and not export_q:
        scratch = q_shapes + scratch
    if k_parts is not None:
        scratch.append(pltpu.VMEM((keys, 2 * DIM), f32))
    given = (q_parts is not None, k_parts is not None)
    cfg = (start, count, sets, given, finals, raws, 0 if oldq is None else units, export_q)

    def body(*refs):
        tile_kernel(cfg, *refs)

    return pl.pallas_call(
        body,
        in_specs=[smem] + [vmem] * len(arrays),
        out_specs=[vmem] * len(outs),
        out_shape=outs,
        scratch_shapes=scratch,
        compiler_params=pltpu.CompilerParams(vmem_limit_bytes=20 << 20),
    )(tab, *[in_vmem(v) for v in arrays])


def finish_kernel(parts, key_ref, value_ref):
    total = jnp.sum(parts[...].astype(f32), axis=0)
    key_ref[...] = (total[:, :DIM] * DIM ** (-0.5)).astype(bf16)
    value_ref[...] = total[:, DIM:].astype(bf16)


def unit_low(value, fold, fill):
    lane = lax.broadcasted_iota(jnp.int32, value.shape, 1)
    first = fold(jnp.where(lane < UNIT, value, fill), axis=1, keepdims=True)
    second = fold(jnp.where(lane < UNIT, fill, value), axis=1, keepdims=True)
    return first, second


def plan_kernel(table, position, modality, tab, kcode, qlim, rows, sems):
    y, zlo, core, x, zhh, zhl = (lax.axis_index(a) for a in AXES)

    def line(y, zlo, core, zhl):
        return ((((y * 2 + zlo) * 2 + core) * 4 + x) * 2 + zhh) * 2 + zhl

    lines = [line(b, zlo, core ^ s, zhl) for s in range(2) for b in range(NY)]
    lines += [line(y, zlo ^ (mask >> 1), core, zhl ^ (mask & 1)) for mask in MASKS]
    moves = []
    for i, at in enumerate(lines):
        for j, ref in enumerate((position, modality)):
            moves.append(pltpu.make_async_copy(ref.at[at], rows.at[j, i], sems.at[j, i]))
    for move in moves:
        move.start()
    for move in moves:
        move.wait()
    pos = jnp.concatenate([rows[0, i] for i in range(len(lines))], axis=0)
    mod = jnp.concatenate([rows[1, i] for i in range(len(lines))], axis=0)
    keys = 2 * NY
    kcode[...] = pos[:keys] * 4 + mod[:keys]
    low = unit_low(pos[:keys], jnp.min, 1 << 20)
    high = unit_low(pos[keys:], jnp.max, -1)
    qlast = jnp.concatenate(
        [high[half][a : a + 1] for a in range(NZ) for half in range(2)], axis=0
    )
    qlast = jnp.concatenate([qlast, jnp.zeros((TOK - QUNITS, 1), jnp.int32)], axis=0)
    qlast = jnp.broadcast_to(qlast, (TOK, TOK)).T[:KUNITS] >> 6
    lane = lax.broadcasted_iota(jnp.int32, (KUNITS, TOK), 1)
    index = lax.broadcasted_iota(jnp.int32, (KUNITS, TOK), 0)
    for s in range(2):
        part = slice(s * NY, (s + 1) * NY)
        column = jnp.broadcast_to(jnp.concatenate([low[0][part], low[1][part]], axis=0), (KUNITS, TOK))
        square = jnp.concatenate([column, jnp.zeros((TOK - KUNITS, TOK), jnp.int32)], axis=0).T
        across = square[:KUNITS]
        before = (column < across) | ((column == across) & (index < lane))
        tab[s : s + 1, :] = jnp.sum(before.astype(jnp.int32), axis=0, keepdims=True)
        seen = (column >> 6) <= qlast
        tab[2 + s : 3 + s, :] = jnp.sum(seen.astype(jnp.int32), axis=0, keepdims=True)
    qpos, qmod = pos[keys:], mod[keys:]
    for m in range(3):
        bid = jnp.where(qmod == 0, table[0, m], jnp.where(qmod == 1, table[1, m], table[2, m]))
        lim = jnp.where(bid == 1, qpos | (UNIT - 1), qpos)
        for a in range(NZ):
            for half in range(2):
                cut = lim[a : a + 1, half * UNIT : (half + 1) * UNIT]
                qlim[2 * a + half, m : m + 1, :] = jnp.concatenate([cut] * HEADS, axis=1)


def plan(position, modality, table):
    hbm = pl.BlockSpec(memory_space=pltpu.HBM)
    vmem = pl.BlockSpec(memory_space=pltpu.VMEM)
    count = 2 * NY + NZ
    lines = position.shape[0] // TOK
    return pl.pallas_call(
        plan_kernel,
        in_specs=[pl.BlockSpec(memory_space=pltpu.SMEM), hbm, hbm],
        out_specs=[vmem] * 3,
        out_shape=[
            jax.ShapeDtypeStruct((4, TOK), jnp.int32),
            pltpu.VMEM((2 * NY, TOK), jnp.int32),
            pltpu.VMEM((QUNITS, 3, ROWS), jnp.int32),
        ],
        scratch_shapes=[
            pltpu.VMEM((2, count, 1, TOK), jnp.int32),
            pltpu.SemaphoreType.DMA((2, count)),
        ],
        compiler_params=pltpu.CompilerParams(vmem_limit_bytes=8 << 20),
        name="plan",
    )(
        table,
        pltpu.with_memory_space_constraint(position.reshape(lines, 1, TOK), pltpu.HBM),
        pltpu.with_memory_space_constraint(modality.reshape(lines, 1, TOK), pltpu.HBM),
    )


def shards(queries, grad_out, attn_out, key_states, value_states, log_norm, position, modality, table):
    def along_z(value, mask):
        return lax.ppermute(value, ("zlo", "zhl"), [(i, i ^ mask) for i in range(NZ)])

    def other_core(value):
        return lax.ppermute(value, "core", [(0, 1), (1, 0)])

    def over_y(value):
        return lax.all_to_all(value, "y", 0, 0)

    pair = jnp.concatenate([key_states, value_states], axis=1)
    copies = jnp.broadcast_to(pair[None], (NY, TOK, 2 * DIM))
    msg = pl.pallas_call(
        pack_kernel, out_shape=pltpu.VMEM((TOK + 8, 2 * WIDE), bf16), compiler_params=pltpu.CompilerParams(vmem_limit_bytes=8 << 20), name="pack"
    )(queries, grad_out, attn_out, log_norm.T)
    kvo = over_y(copies).reshape(NY * TOK, 2 * DIM)
    far = along_z(msg, 1)
    near = along_z(msg, 2)
    tab, kcode, qlim = plan(position, modality, table)
    kvx = other_core(kvo)
    last = along_z(far, 2)
    own_q, near_q, far_q, old, *k_parts = tile(
        tab, 0, (0, 1), qlim, (msg, near, far), (kvo, kvx), kcode,
        finals=((0, f32), (1, bf16), (2, bf16)),
    )
    raw_last, gkvx, *q_parts = tile(
        tab, 3, (1,), qlim, (last,), k_parts=k_parts, raws=(0, 2), old=old, out_type=bf16,
        export_q=True,
    )
    got = other_core(gkvx)
    last_q, gkvo = tile(
        tab, 3, (0,), qlim, q_parts=q_parts, k_parts=k_parts, finals=((0, bf16),),
        oldq=raw_last, old=old,
    )
    paired = (gkvo + got.astype(f32)).astype(bf16).reshape(NY, TOK, 2 * DIM)
    summed = over_y(paired)
    narrow = jax.ShapeDtypeStruct((TOK, DIM), bf16)
    grad_key, grad_value = pl.pallas_call(
        finish_kernel, out_shape=[narrow] * 2, compiler_params=pltpu.CompilerParams(vmem_limit_bytes=8 << 20), name="finish"
    )(in_vmem(summed))
    back = [along_z(g, mask) for g, mask in zip((near_q, far_q, last_q), MASKS[1:])]
    grad_q = (own_q + back[0].astype(f32) + back[1].astype(f32) + back[2].astype(f32)) * DIM ** (-0.5)
    return grad_q.astype(bf16), grad_key, grad_value


def solution(mesh):
    fine = Mesh(mesh.devices.reshape(8, 2, 2, 4, 2, 2), AXES)
    tokens = P(AXES, None)

    return jax.shard_map(
        shards,
        mesh=fine,
        in_specs=(tokens,) * 6 + (P(), P(), P()),
        out_specs=(tokens,) * 3,
        check_vma=False,
    )
```

```python
import jax
import jax.numpy as jnp
from jax import lax
from jax.experimental import pallas as pl
from jax.experimental.pallas import tpu as pltpu
from jax.sharding import Mesh, PartitionSpec as P

UNIT = 64
TOK = 128
HEADS = 4
DIM = 128
WIDE = HEADS * DIM
NZ = 4
NY = 8
QUNITS = 2 * NZ
KUNITS = NY * TOK // UNIT
GROUP = 8
PAR = 3
MASKS = (0, 2, 1, 3)
ROWS = HEADS * UNIT
AXES = ("y", "zlo", "core", "x", "zhh", "zhl")
bf16 = jnp.bfloat16
f32 = jnp.float32


def pack_kernel(q_ref, d_ref, o_ref, lse_ref, msg_ref):
    msg_ref[:TOK, :WIDE] = q_ref[...]
    msg_ref[:TOK, WIDE:] = d_ref[...]
    lane = lax.broadcasted_iota(jnp.int32, (TOK, DIM), 1)
    delta = jnp.zeros((TOK, DIM), f32)
    for h in range(HEADS):
        cut = slice(h * DIM, (h + 1) * DIM)
        column = jnp.sum(d_ref[:, cut].astype(f32) * o_ref[:, cut].astype(f32), axis=1, keepdims=True)
        delta = jnp.where(lane == h, column, delta)
    delta = delta.T
    line = [lse_ref[h : h + 1, :] for h in range(HEADS)] + [delta[h : h + 1, :] for h in range(HEADS)]
    rest = jnp.concatenate(line, axis=1)
    parts = []
    for _ in range(3):
        low = rest.astype(bf16).astype(f32)
        parts.append(low)
        rest = rest - low
    parts.append(jnp.zeros((5, 2 * WIDE), f32))
    msg_ref[TOK:, :] = jnp.concatenate(parts, axis=0).astype(bf16)


def nt(left, right):
    return lax.dot_general(left, right, (((1,), (1,)), ((), ())), preferred_element_type=f32)


def nn(left, right):
    return lax.dot_general(left, right, (((1,), (0,)), ((), ())), preferred_element_type=f32)


def tile_kernel(cfg, *refs):
    it = iter(refs)

    def take(n):
        return [next(it) for _ in range(n)]

    start, count, sets, given, finals, raws, old_units, export_q = cfg
    q_given, k_given = given
    spread_out = k_given
    tab = next(it)
    msgs = [] if q_given else take(count)
    kvs = [] if k_given else take(len(sets))
    kcode = None if k_given else next(it)
    qlim = next(it)
    q_parts = take(4) if q_given else None
    k_parts = take(3) if k_given else None
    oldq = next(it) if old_units else None
    old = next(it) if k_given else None
    gqs = take(len(finals))
    rawq = next(it) if raws else None
    out = next(it)
    if q_parts is None and export_q:
        q_parts = take(4)
    if k_parts is None:
        k_parts = take(3)
    if q_parts is None:
        q_parts = take(4)
    gq, work = take(2)
    acc = next(it) if spread_out else out
    qs, ds, lse, delta = q_parts
    ks, kt, kc = k_parts
    base = 2 * start
    units = 2 * count
    chunks = KUNITS // GROUP
    keys = KUNITS * UNIT
    span = GROUP * UNIT
    chunk0 = sets[0] * chunks
    filled = jnp.int32(0)
    for which, s in enumerate(sets):
        for u in range(units):
            for c in range(chunks):
                work[filled] = (which * chunks + c) * units + u
                active = c * GROUP < tab[2 + s, base + u]
                filled = filled + active.astype(jnp.int32)
    rounds = (filled + PAR - 1) // PAR
    for a, m in enumerate(msgs):
        meta = m[TOK : TOK + 8, :].astype(f32)
        meta = meta[0:1] + meta[1:2] + meta[2:3]
        for half in range(2):
            u = 2 * a + half
            rows = slice(half * UNIT, (half + 1) * UNIT)
            for h in range(HEADS):
                dst = slice(u * ROWS + h * UNIT, u * ROWS + (h + 1) * UNIT)
                qs[dst, :] = m[rows, h * DIM : (h + 1) * DIM]
                ds[dst, :] = m[rows, WIDE + h * DIM : WIDE + (h + 1) * DIM]
            for ref, first in ((lse, 0), (delta, WIDE)):
                cuts = [first + h * TOK + half * UNIT for h in range(HEADS)]
                ref[u] = jnp.concatenate([meta[:, c : c + UNIT] for c in cuts], axis=1)
    gq[...] = jnp.zeros_like(gq) if oldq is None else oldq[...]
    if old is None:
        acc[...] = jnp.zeros_like(acc)
    else:
        acc[...] = old[sets[0] * keys : (sets[0] + 1) * keys, :]
    spots = []
    for which, s in enumerate(sets):
        for b in range(NY):
            if not k_given:
                row = kcode[s * NY + b : s * NY + b + 1, :]
                wide = jnp.broadcast_to(row, (TOK, TOK)).T
            for half in range(2):
                at = tab[s, half * NY + b] + which * KUNITS
                spot = pl.multiple_of(at * UNIT, UNIT)
                nat = slice(b * TOK + half * UNIT, b * TOK + (half + 1) * UNIT)
                spots.append((nat, spot))
                if not k_given:
                    ks[pl.ds(spot, UNIT), :] = kvs[which][nat, :]
                    kc[pl.ds(spot, UNIT), :] = wide[half * UNIT : (half + 1) * UNIT]
    if not k_given:
        for c in range(chunks * len(sets)):
            kt[c] = ks[c * span : (c + 1) * span, :DIM].astype(f32).T.astype(bf16)
    score_scale = DIM ** (-0.5)

    def item(index):
        code = jnp.where(index < filled, work[jnp.minimum(index, filled - 1)], 0)
        u = code % units
        c = code // units
        spot = pl.ds(pl.multiple_of(c * span, span), span)
        where_ = pl.ds(pl.multiple_of((chunk0 + c) * span, span), span)
        keys, vals = ks[where_, :DIM], ks[where_, DIM:]
        at = pl.ds(pl.multiple_of(u * ROWS, ROWS), ROWS)
        q, d = qs[at, :], ds[at, :]
        probs = jnp.exp(nt(keys, q) * score_scale - lse[u])
        kcodes = kc[where_, :]
        mod, pos = kcodes & 3, kcodes >> 2
        lim = jnp.where(index < filled, qlim[base + u], -1)
        bands = []
        for cut in (slice(0, DIM), slice(DIM, ROWS)):
            bound = jnp.where(mod == 0, lim[0:1, cut], jnp.where(mod == 1, lim[1:2, cut], lim[2:3, cut]))
            bands.append(jnp.where(pos <= bound, probs[:, cut], 0.0))
        probs = jnp.concatenate(bands, axis=1)
        grads = probs * (nt(vals, d) - delta[u])
        plow = probs.astype(bf16)
        glow = grads.astype(bf16)
        acc[spot, DIM:] += nn(plow, d)
        acc[spot, :DIM] += nn(glow, q)
        gq[u] += nn(kt[chunk0 + c], glow)

    def body(r, _):
        for j in range(PAR):
            item(r * PAR + j)
        return 0

    lax.fori_loop(0, rounds, body, 0)
    if spread_out:
        for nat, spot in spots:
            out[nat, :] = acc[pl.ds(spot, UNIT), :].astype(out.dtype)
    if rawq is not None:
        rawq[...] = gq[raws[0] : raws[1]]
    for (a, _), g in zip(finals, gqs):
        for half in range(2):
            rows = slice(half * UNIT, (half + 1) * UNIT)
            whole = gq[2 * a + half].T
            for h in range(HEADS):
                part = whole[h * UNIT : (h + 1) * UNIT, :]
                g[rows, h * DIM : (h + 1) * DIM] = part.astype(g.dtype)


def in_vmem(value):
    return pltpu.with_memory_space_constraint(value, pltpu.VMEM)


def tile(tab, start, sets, qlim, msgs=(), kvs=(), kcode=None, q_parts=None, k_parts=None, finals=(),
         raws=None, oldq=None, old=None, out_type=f32, export_q=False):
    count = q_parts[2].shape[0] // 2 if q_parts is not None else len(msgs)
    units = 2 * count
    keys = len(sets) * KUNITS * UNIT
    smem = pl.BlockSpec(memory_space=pltpu.SMEM)
    vmem = pl.BlockSpec(memory_space=pltpu.VMEM)
    arrays = [*msgs, *kvs] + ([] if kcode is None else [kcode]) + [qlim]
    arrays += [*(q_parts or ()), *(k_parts or ())] + [v for v in (oldq, old) if v is not None]
    q_shapes = [
        pltpu.VMEM((units * ROWS, DIM), bf16),
        pltpu.VMEM((units * ROWS, DIM), bf16),
        pltpu.VMEM((units, 1, ROWS), f32),
        pltpu.VMEM((units, 1, ROWS), f32),
    ]
    k_shapes = [
        pltpu.VMEM((keys, 2 * DIM), bf16),
        pltpu.VMEM((keys // (GROUP * UNIT), DIM, GROUP * UNIT), bf16),
        pltpu.VMEM((keys, DIM), jnp.int32),
    ]
    outs = [pltpu.VMEM((TOK, WIDE), t) for _, t in finals]
    if raws:
        outs.append(pltpu.VMEM((raws[1] - raws[0], DIM, ROWS), f32))
    outs.append(pltpu.VMEM((keys, 2 * DIM), out_type))
    if q_parts is None and export_q:
        outs += q_shapes
    if k_parts is None:
        outs += k_shapes
    scratch = [
        pltpu.VMEM((units, DIM, ROWS), f32),
        pltpu.SMEM((units * len(sets) * (KUNITS // GROUP) + 1,), jnp.int32),
    ]
    if q_parts is None and not export_q:
        scratch = q_shapes + scratch
    if k_parts is not None:
        scratch.append(pltpu.VMEM((keys, 2 * DIM), f32))
    given = (q_parts is not None, k_parts is not None)
    cfg = (start, count, sets, given, finals, raws, 0 if oldq is None else units, export_q)

    def body(*refs):
        tile_kernel(cfg, *refs)

    return pl.pallas_call(
        body,
        in_specs=[smem] + [vmem] * len(arrays),
        out_specs=[vmem] * len(outs),
        out_shape=outs,
        scratch_shapes=scratch,
        compiler_params=pltpu.CompilerParams(vmem_limit_bytes=20 << 20),
    )(tab, *[in_vmem(v) for v in arrays])


def copies_kernel(key_ref, value_ref, out, sems):
    moves = []
    for i in range(NY):
        for j, ref in enumerate((key_ref, value_ref)):
            half = out.at[i, :, j * DIM : (j + 1) * DIM]
            moves.append(pltpu.make_async_copy(ref, half, sems.at[2 * i + j]))
    for move in moves:
        move.start()
    for move in moves:
        move.wait()


def finish_kernel(parts, key_ref, value_ref):
    total = jnp.sum(parts[...].astype(f32), axis=0)
    key_ref[...] = (total[:, :DIM] * DIM ** (-0.5)).astype(bf16)
    value_ref[...] = total[:, DIM:].astype(bf16)


def unit_low(value, fold, fill):
    lane = lax.broadcasted_iota(jnp.int32, value.shape, 1)
    first = fold(jnp.where(lane < UNIT, value, fill), axis=1, keepdims=True)
    second = fold(jnp.where(lane < UNIT, fill, value), axis=1, keepdims=True)
    return first, second


def plan_kernel(table, position, modality, tab, kcode, qlim, rows, sems):
    y, zlo, core, x, zhh, zhl = (lax.axis_index(a) for a in AXES)

    def line(y, zlo, core, zhl):
        return ((((y * 2 + zlo) * 2 + core) * 4 + x) * 2 + zhh) * 2 + zhl

    lines = [line(b, zlo, core ^ s, zhl) for s in range(2) for b in range(NY)]
    lines += [line(y, zlo ^ (mask >> 1), core, zhl ^ (mask & 1)) for mask in MASKS]
    moves = []
    for i, at in enumerate(lines):
        for j, ref in enumerate((position, modality)):
            moves.append(pltpu.make_async_copy(ref.at[at], rows.at[j, i], sems.at[j, i]))
    for move in moves:
        move.start()
    for move in moves:
        move.wait()
    pos = jnp.concatenate([rows[0, i] for i in range(len(lines))], axis=0)
    mod = jnp.concatenate([rows[1, i] for i in range(len(lines))], axis=0)
    keys = 2 * NY
    kcode[...] = pos[:keys] * 4 + mod[:keys]
    low = unit_low(pos[:keys], jnp.min, 1 << 20)
    high = unit_low(pos[keys:], jnp.max, -1)
    qlast = jnp.concatenate(
        [high[half][a : a + 1] for a in range(NZ) for half in range(2)], axis=0
    )
    qlast = jnp.concatenate([qlast, jnp.zeros((TOK - QUNITS, 1), jnp.int32)], axis=0)
    qlast = jnp.broadcast_to(qlast, (TOK, TOK)).T[:KUNITS] >> 6
    lane = lax.broadcasted_iota(jnp.int32, (KUNITS, TOK), 1)
    index = lax.broadcasted_iota(jnp.int32, (KUNITS, TOK), 0)
    for s in range(2):
        part = slice(s * NY, (s + 1) * NY)
        column = jnp.broadcast_to(jnp.concatenate([low[0][part], low[1][part]], axis=0), (KUNITS, TOK))
        square = jnp.concatenate([column, jnp.zeros((TOK - KUNITS, TOK), jnp.int32)], axis=0).T
        across = square[:KUNITS]
        before = (column < across) | ((column == across) & (index < lane))
        tab[s : s + 1, :] = jnp.sum(before.astype(jnp.int32), axis=0, keepdims=True)
        seen = (column >> 6) <= qlast
        tab[2 + s : 3 + s, :] = jnp.sum(seen.astype(jnp.int32), axis=0, keepdims=True)
    qpos, qmod = pos[keys:], mod[keys:]
    for m in range(3):
        bid = jnp.where(qmod == 0, table[0, m], jnp.where(qmod == 1, table[1, m], table[2, m]))
        lim = jnp.where(bid == 1, qpos | (UNIT - 1), qpos)
        for a in range(NZ):
            for half in range(2):
                cut = lim[a : a + 1, half * UNIT : (half + 1) * UNIT]
                qlim[2 * a + half, m : m + 1, :] = jnp.concatenate([cut] * HEADS, axis=1)


def plan(position, modality, table):
    hbm = pl.BlockSpec(memory_space=pltpu.HBM)
    vmem = pl.BlockSpec(memory_space=pltpu.VMEM)
    count = 2 * NY + NZ
    lines = position.shape[0] // TOK
    return pl.pallas_call(
        plan_kernel,
        in_specs=[pl.BlockSpec(memory_space=pltpu.SMEM), hbm, hbm],
        out_specs=[vmem] * 3,
        out_shape=[
            jax.ShapeDtypeStruct((4, TOK), jnp.int32),
            pltpu.VMEM((2 * NY, TOK), jnp.int32),
            pltpu.VMEM((QUNITS, 3, ROWS), jnp.int32),
        ],
        scratch_shapes=[
            pltpu.VMEM((2, count, 1, TOK), jnp.int32),
            pltpu.SemaphoreType.DMA((2, count)),
        ],
        compiler_params=pltpu.CompilerParams(vmem_limit_bytes=8 << 20),
        name="plan",
    )(
        table,
        pltpu.with_memory_space_constraint(position.reshape(lines, 1, TOK), pltpu.HBM),
        pltpu.with_memory_space_constraint(modality.reshape(lines, 1, TOK), pltpu.HBM),
    )


def shards(queries, grad_out, attn_out, key_states, value_states, log_norm, position, modality, table):
    def along_z(value, mask):
        return lax.ppermute(value, ("zlo", "zhl"), [(i, i ^ mask) for i in range(NZ)])

    def other_core(value):
        return lax.ppermute(value, "core", [(0, 1), (1, 0)])

    def over_y(value):
        return lax.all_to_all(value, "y", 0, 0)

    hbm = pl.BlockSpec(memory_space=pltpu.HBM)
    copies = pl.pallas_call(
        copies_kernel,
        out_shape=jax.ShapeDtypeStruct((NY, TOK, 2 * DIM), bf16),
        in_specs=[hbm] * 2,
        out_specs=hbm,
        scratch_shapes=[pltpu.SemaphoreType.DMA((2 * NY,))],
        compiler_params=pltpu.CompilerParams(vmem_limit_bytes=8 << 20),
        name="copies",
    )(
        pltpu.with_memory_space_constraint(key_states, pltpu.HBM),
        pltpu.with_memory_space_constraint(value_states, pltpu.HBM),
    )
    msg = pl.pallas_call(
        pack_kernel, out_shape=pltpu.VMEM((TOK + 8, 2 * WIDE), bf16), compiler_params=pltpu.CompilerParams(vmem_limit_bytes=8 << 20), name="pack"
    )(queries, grad_out, attn_out, log_norm.T)
    kvo = over_y(copies).reshape(NY * TOK, 2 * DIM)
    far = along_z(msg, 1)
    near = along_z(msg, 2)
    tab, kcode, qlim = plan(position, modality, table)
    kvx = other_core(kvo)
    last = along_z(far, 2)
    own_q, near_q, far_q, old, *k_parts = tile(
        tab, 0, (0, 1), qlim, (msg, near, far), (kvo, kvx), kcode,
        finals=((0, f32), (1, bf16), (2, bf16)),
    )
    raw_last, gkvx, *q_parts = tile(
        tab, 3, (1,), qlim, (last,), k_parts=k_parts, raws=(0, 2), old=old, out_type=bf16,
        export_q=True,
    )
    got = other_core(gkvx)
    last_q, gkvo = tile(
        tab, 3, (0,), qlim, q_parts=q_parts, k_parts=k_parts, finals=((0, bf16),),
        oldq=raw_last, old=old,
    )
    paired = (gkvo + got.astype(f32)).astype(bf16).reshape(NY, TOK, 2 * DIM)
    summed = over_y(paired)
    narrow = jax.ShapeDtypeStruct((TOK, DIM), bf16)
    grad_key, grad_value = pl.pallas_call(
        finish_kernel, out_shape=[narrow] * 2, compiler_params=pltpu.CompilerParams(vmem_limit_bytes=8 << 20), name="finish"
    )(in_vmem(summed))
    back = []
    for part, mask in ((last_q, 3), (far_q, 1), (near_q, 2)):
        back.append(along_z(part, mask).astype(f32))
    grad_q = (own_q + back[2] + back[1] + back[0]) * DIM ** (-0.5)
    return grad_q.astype(bf16), grad_key, grad_value


def solution(mesh):
    fine = Mesh(mesh.devices.reshape(8, 2, 2, 4, 2, 2), AXES)
    tokens = P(AXES, None)

    return jax.shard_map(
        shards,
        mesh=fine,
        in_specs=(tokens,) * 6 + (P(), P(), P()),
        out_specs=(tokens,) * 3,
        check_vma=False,
    )
```

```python
import jax
import jax.numpy as jnp
from jax import lax
from jax.experimental import pallas as pl
from jax.experimental.pallas import tpu as pltpu
from jax.sharding import Mesh, PartitionSpec as P

UNIT = 64
TOK = 128
HEADS = 4
DIM = 128
WIDE = HEADS * DIM
NZ = 4
NY = 8
QUNITS = 2 * NZ
KUNITS = NY * TOK // UNIT
GROUP = 8
PAR = 3
MASKS = (0, 2, 1, 3)
ROWS = HEADS * UNIT
AXES = ("y", "zlo", "core", "x", "zhh", "zhl")
bf16 = jnp.bfloat16
f32 = jnp.float32


def pack_kernel(q_ref, d_ref, o_ref, lse_ref, msg_ref):
    msg_ref[:TOK, :WIDE] = q_ref[...]
    msg_ref[:TOK, WIDE:] = d_ref[...]
    lane = lax.broadcasted_iota(jnp.int32, (TOK, DIM), 1)
    delta = jnp.zeros((TOK, DIM), f32)
    for h in range(HEADS):
        cut = slice(h * DIM, (h + 1) * DIM)
        column = jnp.sum(d_ref[:, cut].astype(f32) * o_ref[:, cut].astype(f32), axis=1, keepdims=True)
        delta = jnp.where(lane == h, column, delta)
    delta = delta.T
    line = [lse_ref[h : h + 1, :] for h in range(HEADS)] + [delta[h : h + 1, :] for h in range(HEADS)]
    rest = jnp.concatenate(line, axis=1)
    parts = []
    for _ in range(3):
        low = rest.astype(bf16).astype(f32)
        parts.append(low)
        rest = rest - low
    parts.append(jnp.zeros((5, 2 * WIDE), f32))
    msg_ref[TOK:, :] = jnp.concatenate(parts, axis=0).astype(bf16)


def nt(left, right):
    return lax.dot_general(left, right, (((1,), (1,)), ((), ())), preferred_element_type=f32)


def nn(left, right):
    return lax.dot_general(left, right, (((1,), (0,)), ((), ())), preferred_element_type=f32)


def tile_kernel(cfg, *refs):
    it = iter(refs)

    def take(n):
        return [next(it) for _ in range(n)]

    start, count, sets, given, finals, raws, old_units, export_q = cfg
    q_given, k_given = given
    spread_out = k_given
    tab = next(it)
    msgs = [] if q_given else take(count)
    kvs = [] if k_given else take(len(sets))
    kcode = None if k_given else next(it)
    qlim = next(it)
    q_parts = take(4) if q_given else None
    k_parts = take(3) if k_given else None
    oldq = next(it) if old_units else None
    old = next(it) if k_given else None
    gqs = take(len(finals))
    rawq = next(it) if raws else None
    out = next(it)
    if q_parts is None and export_q:
        q_parts = take(4)
    if k_parts is None:
        k_parts = take(3)
    if q_parts is None:
        q_parts = take(4)
    gq, work = take(2)
    acc = next(it) if spread_out else out
    qs, ds, lse, delta = q_parts
    ks, kt, kc = k_parts
    base = 2 * start
    units = 2 * count
    chunks = KUNITS // GROUP
    keys = KUNITS * UNIT
    span = GROUP * UNIT
    chunk0 = sets[0] * chunks
    filled = jnp.int32(0)
    for which, s in enumerate(sets):
        for u in range(units):
            for c in range(chunks):
                work[filled] = (which * chunks + c) * units + u
                active = c * GROUP < tab[2 + s, base + u]
                filled = filled + active.astype(jnp.int32)
    rounds = (filled + PAR - 1) // PAR
    for a, m in enumerate(msgs):
        meta = m[TOK : TOK + 8, :].astype(f32)
        meta = meta[0:1] + meta[1:2] + meta[2:3]
        for half in range(2):
            u = 2 * a + half
            rows = slice(half * UNIT, (half + 1) * UNIT)
            for h in range(HEADS):
                dst = slice(u * ROWS + h * UNIT, u * ROWS + (h + 1) * UNIT)
                qs[dst, :] = m[rows, h * DIM : (h + 1) * DIM]
                ds[dst, :] = m[rows, WIDE + h * DIM : WIDE + (h + 1) * DIM]
            for ref, first in ((lse, 0), (delta, WIDE)):
                cuts = [first + h * TOK + half * UNIT for h in range(HEADS)]
                ref[u] = jnp.concatenate([meta[:, c : c + UNIT] for c in cuts], axis=1)
    gq[...] = jnp.zeros_like(gq) if oldq is None else oldq[...]
    if old is None:
        acc[...] = jnp.zeros_like(acc)
    else:
        acc[...] = old[sets[0] * keys : (sets[0] + 1) * keys, :]
    spots = []
    for which, s in enumerate(sets):
        for b in range(NY):
            if not k_given:
                row = kcode[s * NY + b : s * NY + b + 1, :]
                wide = jnp.broadcast_to(row, (TOK, TOK)).T
            for half in range(2):
                at = tab[s, half * NY + b] + which * KUNITS
                spot = pl.multiple_of(at * UNIT, UNIT)
                nat = slice(b * TOK + half * UNIT, b * TOK + (half + 1) * UNIT)
                spots.append((nat, spot))
                if not k_given:
                    ks[pl.ds(spot, UNIT), :] = kvs[which][nat, :]
                    kc[pl.ds(spot, UNIT), :] = wide[half * UNIT : (half + 1) * UNIT]
    if not k_given:
        for c in range(chunks * len(sets)):
            kt[c] = ks[c * span : (c + 1) * span, :DIM].astype(f32).T.astype(bf16)
    score_scale = DIM ** (-0.5)

    def item(index):
        code = jnp.where(index < filled, work[jnp.minimum(index, filled - 1)], 0)
        u = code % units
        c = code // units
        spot = pl.ds(pl.multiple_of(c * span, span), span)
        where_ = pl.ds(pl.multiple_of((chunk0 + c) * span, span), span)
        keys, vals = ks[where_, :DIM], ks[where_, DIM:]
        at = pl.ds(pl.multiple_of(u * ROWS, ROWS), ROWS)
        q, d = qs[at, :], ds[at, :]
        probs = jnp.exp(nt(keys, q) * score_scale - lse[u])
        kcodes = kc[where_, :]
        mod, pos = kcodes & 3, kcodes >> 2
        lim = jnp.where(index < filled, qlim[base + u], -1)
        bands = []
        for cut in (slice(0, DIM), slice(DIM, ROWS)):
            bound = jnp.where(mod == 0, lim[0:1, cut], jnp.where(mod == 1, lim[1:2, cut], lim[2:3, cut]))
            bands.append(jnp.where(pos <= bound, probs[:, cut], 0.0))
        probs = jnp.concatenate(bands, axis=1)
        grads = probs * (nt(vals, d) - delta[u])
        plow = probs.astype(bf16)
        glow = grads.astype(bf16)
        acc[spot, DIM:] += nn(plow, d)
        acc[spot, :DIM] += nn(glow, q)
        gq[u] += nn(kt[chunk0 + c], glow)

    def body(r, _):
        for j in range(PAR):
            item(r * PAR + j)
        return 0

    lax.fori_loop(0, rounds, body, 0)
    if spread_out:
        for nat, spot in spots:
            out[nat, :] = acc[pl.ds(spot, UNIT), :].astype(out.dtype)
    if rawq is not None:
        rawq[...] = gq[raws[0] : raws[1]]
    for (a, _), g in zip(finals, gqs):
        for half in range(2):
            rows = slice(half * UNIT, (half + 1) * UNIT)
            whole = gq[2 * a + half].T
            for h in range(HEADS):
                part = whole[h * UNIT : (h + 1) * UNIT, :]
                g[rows, h * DIM : (h + 1) * DIM] = part.astype(g.dtype)


def in_vmem(value):
    return pltpu.with_memory_space_constraint(value, pltpu.VMEM)


def tile(tab, start, sets, qlim, msgs=(), kvs=(), kcode=None, q_parts=None, k_parts=None, finals=(),
         raws=None, oldq=None, old=None, out_type=f32, export_q=False):
    count = q_parts[2].shape[0] // 2 if q_parts is not None else len(msgs)
    units = 2 * count
    keys = len(sets) * KUNITS * UNIT
    smem = pl.BlockSpec(memory_space=pltpu.SMEM)
    vmem = pl.BlockSpec(memory_space=pltpu.VMEM)
    arrays = [*msgs, *kvs] + ([] if kcode is None else [kcode]) + [qlim]
    arrays += [*(q_parts or ()), *(k_parts or ())] + [v for v in (oldq, old) if v is not None]
    q_shapes = [
        pltpu.VMEM((units * ROWS, DIM), bf16),
        pltpu.VMEM((units * ROWS, DIM), bf16),
        pltpu.VMEM((units, 1, ROWS), f32),
        pltpu.VMEM((units, 1, ROWS), f32),
    ]
    k_shapes = [
        pltpu.VMEM((keys, 2 * DIM), bf16),
        pltpu.VMEM((keys // (GROUP * UNIT), DIM, GROUP * UNIT), bf16),
        pltpu.VMEM((keys, DIM), jnp.int32),
    ]
    outs = [pltpu.VMEM((TOK, WIDE), t) for _, t in finals]
    if raws:
        outs.append(pltpu.VMEM((raws[1] - raws[0], DIM, ROWS), f32))
    outs.append(pltpu.VMEM((keys, 2 * DIM), out_type))
    if q_parts is None and export_q:
        outs += q_shapes
    if k_parts is None:
        outs += k_shapes
    scratch = [
        pltpu.VMEM((units, DIM, ROWS), f32),
        pltpu.SMEM((units * len(sets) * (KUNITS // GROUP) + 1,), jnp.int32),
    ]
    if q_parts is None and not export_q:
        scratch = q_shapes + scratch
    if k_parts is not None:
        scratch.append(pltpu.VMEM((keys, 2 * DIM), f32))
    given = (q_parts is not None, k_parts is not None)
    cfg = (start, count, sets, given, finals, raws, 0 if oldq is None else units, export_q)

    def body(*refs):
        tile_kernel(cfg, *refs)

    return pl.pallas_call(
        body,
        in_specs=[smem] + [vmem] * len(arrays),
        out_specs=[vmem] * len(outs),
        out_shape=outs,
        scratch_shapes=scratch,
        compiler_params=pltpu.CompilerParams(vmem_limit_bytes=20 << 20),
    )(tab, *[in_vmem(v) for v in arrays])


def finish_kernel(parts, key_ref, value_ref):
    total = jnp.sum(parts[...].astype(f32), axis=0)
    key_ref[...] = (total[:, :DIM] * DIM ** (-0.5)).astype(bf16)
    value_ref[...] = total[:, DIM:].astype(bf16)


def unit_low(value, fold, fill):
    lane = lax.broadcasted_iota(jnp.int32, value.shape, 1)
    first = fold(jnp.where(lane < UNIT, value, fill), axis=1, keepdims=True)
    second = fold(jnp.where(lane < UNIT, fill, value), axis=1, keepdims=True)
    return first, second


def plan_kernel(table, position, modality, tab, kcode, qlim, rows, sems):
    y, zlo, core, x, zhh, zhl = (lax.axis_index(a) for a in AXES)

    def line(y, zlo, core, zhl):
        return ((((y * 2 + zlo) * 2 + core) * 4 + x) * 2 + zhh) * 2 + zhl

    lines = [line(b, zlo, core ^ s, zhl) for s in range(2) for b in range(NY)]
    lines += [line(y, zlo ^ (mask >> 1), core, zhl ^ (mask & 1)) for mask in MASKS]
    moves = []
    for i, at in enumerate(lines):
        for j, ref in enumerate((position, modality)):
            moves.append(pltpu.make_async_copy(ref.at[at], rows.at[j, i], sems.at[j, i]))
    for move in moves:
        move.start()
    for move in moves:
        move.wait()
    pos = jnp.concatenate([rows[0, i] for i in range(len(lines))], axis=0)
    mod = jnp.concatenate([rows[1, i] for i in range(len(lines))], axis=0)
    keys = 2 * NY
    kcode[...] = pos[:keys] * 4 + mod[:keys]
    low = unit_low(pos[:keys], jnp.min, 1 << 20)
    high = unit_low(pos[keys:], jnp.max, -1)
    qlast = jnp.concatenate(
        [high[half][a : a + 1] for a in range(NZ) for half in range(2)], axis=0
    )
    qlast = jnp.concatenate([qlast, jnp.zeros((TOK - QUNITS, 1), jnp.int32)], axis=0)
    qlast = jnp.broadcast_to(qlast, (TOK, TOK)).T[:KUNITS] >> 6
    lane = lax.broadcasted_iota(jnp.int32, (KUNITS, TOK), 1)
    index = lax.broadcasted_iota(jnp.int32, (KUNITS, TOK), 0)
    for s in range(2):
        part = slice(s * NY, (s + 1) * NY)
        column = jnp.broadcast_to(jnp.concatenate([low[0][part], low[1][part]], axis=0), (KUNITS, TOK))
        square = jnp.concatenate([column, jnp.zeros((TOK - KUNITS, TOK), jnp.int32)], axis=0).T
        across = square[:KUNITS]
        before = (column < across) | ((column == across) & (index < lane))
        tab[s : s + 1, :] = jnp.sum(before.astype(jnp.int32), axis=0, keepdims=True)
        seen = (column >> 6) <= qlast
        tab[2 + s : 3 + s, :] = jnp.sum(seen.astype(jnp.int32), axis=0, keepdims=True)
    qpos, qmod = pos[keys:], mod[keys:]
    for m in range(3):
        bid = jnp.where(qmod == 0, table[0, m], jnp.where(qmod == 1, table[1, m], table[2, m]))
        lim = jnp.where(bid == 1, qpos | (UNIT - 1), qpos)
        for a in range(NZ):
            for half in range(2):
                cut = lim[a : a + 1, half * UNIT : (half + 1) * UNIT]
                qlim[2 * a + half, m : m + 1, :] = jnp.concatenate([cut] * HEADS, axis=1)


def plan(position, modality, table):
    hbm = pl.BlockSpec(memory_space=pltpu.HBM)
    vmem = pl.BlockSpec(memory_space=pltpu.VMEM)
    count = 2 * NY + NZ
    lines = position.shape[0] // TOK
    return pl.pallas_call(
        plan_kernel,
        in_specs=[pl.BlockSpec(memory_space=pltpu.SMEM), hbm, hbm],
        out_specs=[vmem] * 3,
        out_shape=[
            jax.ShapeDtypeStruct((4, TOK), jnp.int32),
            pltpu.VMEM((2 * NY, TOK), jnp.int32),
            pltpu.VMEM((QUNITS, 3, ROWS), jnp.int32),
        ],
        scratch_shapes=[
            pltpu.VMEM((2, count, 1, TOK), jnp.int32),
            pltpu.SemaphoreType.DMA((2, count)),
        ],
        compiler_params=pltpu.CompilerParams(vmem_limit_bytes=8 << 20),
        name="plan",
    )(
        table,
        pltpu.with_memory_space_constraint(position.reshape(lines, 1, TOK), pltpu.HBM),
        pltpu.with_memory_space_constraint(modality.reshape(lines, 1, TOK), pltpu.HBM),
    )


def shards(queries, grad_out, attn_out, key_states, value_states, log_norm, position, modality, table):
    def along_z(value, mask):
        return lax.ppermute(value, ("zlo", "zhl"), [(i, i ^ mask) for i in range(NZ)])

    def other_core(value):
        return lax.ppermute(value, "core", [(0, 1), (1, 0)])

    def over_y(value):
        return lax.all_to_all(value, "y", 0, 0)

    pair = jnp.concatenate([key_states, value_states], axis=1)
    copies = jnp.broadcast_to(pair[None], (NY, TOK, 2 * DIM))
    msg = pl.pallas_call(
        pack_kernel, out_shape=pltpu.VMEM((TOK + 8, 2 * WIDE), bf16), compiler_params=pltpu.CompilerParams(vmem_limit_bytes=8 << 20), name="pack"
    )(queries, grad_out, attn_out, log_norm.T)
    kvo = over_y(copies).reshape(NY * TOK, 2 * DIM)
    far = along_z(msg, 1)
    near = along_z(msg, 2)
    tab, kcode, qlim = plan(position, modality, table)
    kvx = other_core(kvo)
    last = along_z(far, 2)
    own_q, near_q, far_q, old, *k_parts = tile(
        tab, 0, (0, 1), qlim, (msg, near, far), (kvo, kvx), kcode,
        finals=((0, f32), (1, bf16), (2, bf16)),
    )
    raw_last, gkvx, *q_parts = tile(
        tab, 3, (1,), qlim, (last,), k_parts=k_parts, raws=(0, 2), old=old, out_type=bf16,
        export_q=True,
    )
    got = other_core(gkvx)
    last_q, gkvo = tile(
        tab, 3, (0,), qlim, q_parts=q_parts, k_parts=k_parts, finals=((0, bf16),),
        oldq=raw_last, old=old,
    )
    paired = (gkvo + got.astype(f32)).astype(bf16).reshape(NY, TOK, 2 * DIM)
    summed = over_y(paired)
    narrow = jax.ShapeDtypeStruct((TOK, DIM), bf16)
    grad_key, grad_value = pl.pallas_call(
        finish_kernel, out_shape=[narrow] * 2, compiler_params=pltpu.CompilerParams(vmem_limit_bytes=8 << 20), name="finish"
    )(in_vmem(summed))
    back = []
    for part, mask in ((far_q, 1), (last_q, 3), (near_q, 2)):
        back.append(along_z(part, mask).astype(f32))
    grad_q = (own_q + back[2] + back[1] + back[0]) * DIM ** (-0.5)
    return grad_q.astype(bf16), grad_key, grad_value


def solution(mesh):
    fine = Mesh(mesh.devices.reshape(8, 2, 2, 4, 2, 2), AXES)
    tokens = P(AXES, None)

    return jax.shard_map(
        shards,
        mesh=fine,
        in_specs=(tokens,) * 6 + (P(), P(), P()),
        out_specs=(tokens,) * 3,
        check_vma=False,
    )
```
